32 devices in a mesh: panel: 2 (over core), rad: 4 (over z), hor: 4 (over y, x).
Axes of the slice: x: 2, y: 2, z: 4, core: 2. Of those that a mesh axis runs over, the one named last changes fastest.
Arguments:
- final_cotangent: float32 [2, 8, 4, 32, 2304], P('panel', None, 'rad', 'hor'), may hold values from -6 to 6
- diffusivity: float32 [2, 4, 32, 2304], P('panel', 'rad', 'hor'), may hold values from 0.3 to 1.5
- theta_velocity: float32 [2, 4, 32, 2304], P('panel', 'rad', 'hor'), may hold values from -2.5 to 2.5
- phi_velocity: float32 [2, 4, 32, 2304], P('panel', 'rad', 'hor'), may hold values from -2.5 to 2.5
- radial_stencil: float32 [3, 8, 4], replicated, may hold values from -1 to 1
- field_coupling: float32 [4, 8, 8], replicated, may hold values from -2.5 to 2.5
- slot_targets: int32 [2, 4, 4864], P('panel', 'hor'), may hold values from 0 to 4671, as said below
- slot_donors: int32 [2, 4, 4864], P('panel', 'hor'), may hold values from 0 to 18431, as said below
- slot_weights: float32 [2, 4, 4864], P('panel', 'hor'), may hold values from 0.1 to 0.4
- slot_counts: int32 [2, 4], P('panel', 'hor'), may hold values from 4608 to 4864, as said below
Outputs:
- initial_adjoint: float32 [2, 8, 4, 32, 2304], P('panel', None, 'rad', 'hor')
The draws below stay inside these ranges and needn't reach their ends.
Inputs may be any that keep to these rules, and one draw needn't show every extreme that they name: `slot_targets`: each cell of the first and last rows of a panel is the target of four slots, all in the list of the donor tile s whose index times 2304 / 4 is at most its column and whose next index times 2304 / 4 is above it; each cell of the first and last columns is the target of four slots in the list of one donor tile, and 1 consecutive donor tiles, starting at a tile drawn for each panel, hold these, each for 32 rows in order; live slots come first, the four slots of a cell side by side. `slot_donors`: the four donors of a cell are the corners of a two by two block of cells of one donor tile; for the first cell of every list this block is the tile's last two rows and last two columns. `slot_counts`: A donor tile's list holds 4608 live slots, plus 32 * 8 if it is one of the 1 tiles that hold the first and last columns' cells.
All inputs are finite; a program needn't handle non-finite values.
Results may differ from the reference program's by a relative error of at most 0.00005.
Values sent between devices are 32-bit elements; how exact they have to be, the bound alone decides.
No kernel may reach another device: no remote copies, remote signals or barrier semaphores. Data moves between devices by JAX's collectives and lax.ppermute only.
A program may use at most 128 MiB of HBM per device.

```python
import math
import jax
import jax.numpy as jnp
from jax import lax

FIELDS = 8
ROWS_DEV = 8
PH = 2304
LEVELS = 4
TILES = 4
TH = 32
SLOTS = 4864


def slot_plan(key):
    keys = jax.random.split(jax.random.fold_in(key, 7), 3)
    per_tile = PH // TILES
    band = TILES // 4
    edge_slots = 8 * per_tile
    side_slots = 32 * ROWS_DEV
    band_rows = 4 * ROWS_DEV
    start = jax.random.randint(keys[0], (2, 1), 0, TILES - band + 1).astype(jnp.int32)
    tile = jnp.arange(TILES, dtype=jnp.int32)[None, :]
    in_band = (tile >= start) & (tile < start + band)
    counts = (edge_slots + jnp.where(in_band, side_slots, 0)).astype(jnp.int32)
    slot_ids = jnp.arange(SLOTS, dtype=jnp.int32)[None, None, :]
    cell = slot_ids // 4
    corner = slot_ids % 4
    edge_row = cell // per_tile
    edge_col = tile[..., None] * per_tile + cell % per_tile
    edge_position = edge_row * PH + edge_col
    side_index = (slot_ids - edge_slots) // 4
    side = side_index // band_rows
    global_row = (tile - start)[..., None] * band_rows + side_index % band_rows
    side_position = 2 * PH + side * TH + global_row
    live = slot_ids < counts[..., None]
    targets = jnp.where(live, jnp.where(slot_ids < edge_slots, edge_position, side_position), 0).astype(jnp.int32)
    image_row = jnp.repeat(jax.random.randint(keys[1], (2, TILES, SLOTS // 4), 0, ROWS_DEV - 1), 4, axis=2)
    image_col = jnp.repeat(jax.random.randint(keys[2], (2, TILES, SLOTS // 4), 0, PH - 1), 4, axis=2)
    image_row = jnp.where(slot_ids < 4, ROWS_DEV - 2, image_row).astype(jnp.int32)
    image_col = jnp.where(slot_ids < 4, PH - 2, image_col).astype(jnp.int32)
    donors = jnp.where(live, (image_row + corner // 2) * PH + image_col + corner % 2, 0).astype(jnp.int32)
    return (targets, donors, counts)


def draw_slot_targets(key, part):
    return slot_plan(key)[0]


def draw_slot_donors(key, part):
    return slot_plan(key)[1]


def draw_slot_counts(key, part):
    return slot_plan(key)[2]


def steps_of(own_key, shape, pieces, least, high):
    loudness, own = 1.0, jax.random.fold_in(own_key, 6)
    for axis_at, blocks in pieces:
        steps = jnp.exp(jax.random.uniform(jax.random.fold_in(own, axis_at), (blocks,), jnp.float32, least / len(pieces), high / len(pieces)))
        loudness = loudness * jnp.repeat(steps, shape[axis_at] // blocks).reshape([-1 if axis == axis_at else 1 for axis in range(len(shape))])
    return loudness


def centred(own_key, extent, deviation, most, shards=(), held_as=jnp.bfloat16):
    drawn = deviation * jax.random.normal(own_key, extent, jnp.float32)
    if shards:
        drawn = drawn * steps_of(own_key, extent, shards, -0.22, 0.18)
    return jnp.clip(drawn, -most, most).astype(held_as)


def setup_inputs(seed: int = 0) -> dict:
    seeds = jax.random.split(jax.random.key(seed), 11)
    return {
        "final_cotangent": centred(seeds[0], (2, FIELDS, LEVELS, TH, PH), 1.0, 6.0, ((0, 2), (2, 4), (3, 4)), jnp.float32),
        "diffusivity": jnp.clip(jnp.exp(math.log(1.5) - 1.60943787 * jax.random.uniform(seeds[1], (2, LEVELS, TH, PH), jnp.float32) ** steps_of(seeds[1], (2, LEVELS, TH, PH), ((0, 2), (1, 4), (2, 4)), -0.2, 0.2)), 0.3, 1.5),
        "theta_velocity": centred(seeds[2], (2, LEVELS, TH, PH), 0.5, 2.5, ((0, 2), (1, 4), (2, 4)), jnp.float32),
        "phi_velocity": centred(seeds[3], (2, LEVELS, TH, PH), 0.5, 2.5, ((0, 2), (1, 4), (2, 4)), jnp.float32),
        "radial_stencil": jnp.clip(jax.random.uniform(seeds[4], (3, FIELDS, LEVELS), jnp.float32, -1.0, 1.0), -1.0, 1.0),
        "field_coupling": centred(seeds[5], (LEVELS, FIELDS, FIELDS), 0.35, 2.5, (), jnp.float32),
        "slot_targets": draw_slot_targets(jax.random.fold_in(seeds[10], 71), 0),
        "slot_donors": draw_slot_donors(jax.random.fold_in(seeds[10], 71), 0),
        "slot_weights": jnp.clip(0.1 + 0.3 * jax.random.uniform(seeds[8], (2, TILES, SLOTS), jnp.float32) ** steps_of(seeds[8], (2, TILES, SLOTS), ((0, 2), (1, 4)), -0.2, 0.2), 0.1, 0.4),
        "slot_counts": draw_slot_counts(jax.random.fold_in(seeds[10], 71), 0),
    }


STEP_SIZE = 0.2

def from_lower(field, axis):
    widths = [(0, 0)] * field.ndim
    widths[axis] = (1, 0)
    return lax.slice_in_dim(jnp.pad(field, widths), 0, field.shape[axis], axis=axis)

def from_upper(field, axis):
    widths = [(0, 0)] * field.ndim
    widths[axis] = (0, 1)
    return lax.slice_in_dim(jnp.pad(field, widths), 1, field.shape[axis] + 1, axis=axis)

def operator(state, diffusivity, theta_velocity, phi_velocity, radial_stencil, field_coupling):
    diffuse = diffusivity[:, None]
    theta_flow = theta_velocity[:, None]
    phi_flow = phi_velocity[:, None]
    horizontal = from_lower((diffuse + theta_flow) * state, 3) + from_upper((diffuse - theta_flow) * state, 3)
    horizontal = horizontal + from_lower((diffuse + phi_flow) * state, 4) + from_upper((diffuse - phi_flow) * state, 4)
    horizontal = horizontal - 4.0 * diffuse * state
    diagonal = radial_stencil[0][None, :, :, None, None]
    upper = radial_stencil[1][None, :, :, None, None]
    lower = radial_stencil[2][None, :, :, None, None]
    radial = diagonal * state + upper * from_upper(state, 2) + lower * from_lower(state, 2)
    coupled = jnp.einsum('rfe,perij->pfrij', field_coupling, state, precision=lax.Precision.HIGHEST)
    return horizontal + radial + coupled

def overset(state, border, target_flat, donor_global, live_weights):
    flat = state.reshape(2, FIELDS, LEVELS, TH * PH)
    added = []
    for receiving in range(2):
        donor_panel = 1 - receiving
        values = flat[donor_panel][:, :, donor_global[donor_panel].reshape(-1)] * live_weights[donor_panel].reshape(-1)
        filled = jnp.zeros((FIELDS, LEVELS, TH * PH), jnp.float32).at[:, :, target_flat[donor_panel].reshape(-1)].add(values)
        added.append(filled)
    return jnp.where(border, jnp.float32(0.0), state) + jnp.stack(added).reshape(state.shape)

def reference(final_cotangent, diffusivity, theta_velocity, phi_velocity, radial_stencil, field_coupling, slot_targets, slot_donors, slot_weights, slot_counts):
    row_ids = jnp.arange(TH, dtype=jnp.int32)[:, None]
    col_ids = jnp.arange(PH, dtype=jnp.int32)[None, :]
    border = (row_ids == 0) | (row_ids == TH - 1) | (col_ids == 0) | (col_ids == PH - 1)
    tile_cells = ROWS_DEV * PH
    tile_ids = jnp.arange(TILES, dtype=jnp.int32)
    position = slot_targets.astype(jnp.int32)
    target_row = jnp.where(position < PH, 0, jnp.where(position < 2 * PH, TH - 1, jnp.where(position < 2 * PH + TH, position - 2 * PH, position - 2 * PH - TH))).astype(jnp.int32)
    target_col = jnp.where(position < PH, position, jnp.where(position < 2 * PH, position - PH, jnp.where(position < 2 * PH + TH, 0, PH - 1))).astype(jnp.int32)
    target_flat = (target_row * PH + target_col).astype(jnp.int32)
    donor_global = (tile_ids[None, :, None] * tile_cells + slot_donors).astype(jnp.int32)
    live = jnp.arange(SLOTS, dtype=jnp.int32)[None, None, :] < slot_counts[..., None]
    live_weights = jnp.where(live, slot_weights, jnp.float32(0.0))

    def apply_operator(state):
        return operator(state, diffusivity, theta_velocity, phi_velocity, radial_stencil, field_coupling)

    def apply_overset(state):
        return overset(state, border, target_flat, donor_global, live_weights)

    def forward(initial):
        halfway = apply_overset(initial + 0.5 * STEP_SIZE * apply_operator(initial))
        return apply_overset(initial + STEP_SIZE * apply_operator(halfway))
    _, pullback = jax.vjp(forward, jnp.zeros_like(final_cotangent))
    return pullback(final_cotangent)[0]
```

```python
import functools

import jax
import jax.numpy as jnp
from jax import lax
from jax.experimental import pallas as pl
from jax.experimental.pallas import tpu as pltpu
from jax.sharding import PartitionSpec as P

STEP_SIZE = 0.2
LANES = 128
VMEM = pl.BlockSpec(memory_space=pltpu.VMEM)
SMEM = pl.BlockSpec(memory_space=pltpu.SMEM)


def round_up(n, m):
    return -(-n // m) * m


class Sizes:
    def __init__(self, fields, rows, columns, tiles, slots):
        self.fields, self.rows, self.columns, self.tiles = fields, rows, columns, tiles
        self.chunk = columns // tiles
        self.edge = round_up(self.chunk, LANES)
        self.side = round_up(2 * rows * tiles, LANES)
        self.message = self.side + self.edge
        self.table = self.side + 2 * self.edge
        self.groups = slots // 4
        self.padded = round_up(self.groups, LANES)


def split(x):
    high = x.astype(jnp.bfloat16)
    low = (x - high.astype(jnp.float32)).astype(jnp.bfloat16)
    return high, low


def prepare_kernel(z, target_ref, code_ref, weight_ref, column_ref, pick_ref, place_ref, spread_ref):
    cells = lax.broadcasted_iota(jnp.int32, (z.table, z.padded), 0)
    pick_ref[...] = jnp.where(cells == target_ref[...], 1.0, 0.0).astype(jnp.bfloat16)
    columns = lax.broadcasted_iota(jnp.int32, (z.padded, z.columns), 1)
    place_ref[...] = jnp.where(columns == column_ref[...], 1.0, 0.0).astype(jnp.bfloat16)
    rows = lax.broadcasted_iota(jnp.int32, (z.rows, z.padded), 0)
    for b in range(2):
        total = jnp.zeros((z.rows, z.padded), jnp.float32)
        for q in range(4):
            hit = 2 * rows + b == code_ref[q : q + 1, :]
            total = total + jnp.where(hit, weight_ref[q : q + 1, :], 0.0)
        spread_ref[b] = total


def write_messages(z, tile, state, message_refs):
    first = jnp.concatenate([state[f][0:1, :] for f in range(z.fields)], axis=0)
    last = jnp.concatenate([state[f][z.rows - 1 : z.rows, :] for f in range(z.fields)], axis=0)
    edge = jnp.where(tile == z.tiles - 1, last, first)
    shift = lax.rem(z.columns - tile * z.chunk, z.columns)
    edge = pltpu.roll(edge, shift, 1)
    lane = lax.broadcasted_iota(jnp.int32, (z.rows, LANES), 1)
    row = lax.broadcasted_iota(jnp.int32, (z.rows, LANES), 0)
    sides = []
    for f in range(z.fields):
        left = jnp.where(lane == row, state[f][:, 0:1], 0.0)
        right = jnp.where(lane == row + z.rows, state[f][:, z.columns - 1 : z.columns], 0.0)
        sides.append(jnp.sum(left + right, axis=0, keepdims=True))
    sides = jnp.concatenate(sides, axis=0)
    if z.side > LANES:
        sides = jnp.concatenate([sides, jnp.zeros((z.fields, z.side - LANES), jnp.float32)], axis=1)
    for k, ref in enumerate(message_refs):
        ref[:, 0 : z.side] = pltpu.roll(sides, 2 * z.rows * k, 1) if k else sides
        ref[:, z.side : z.side + z.chunk] = edge[:, k * z.chunk : (k + 1) * z.chunk]
        if z.chunk < z.edge:
            ref[:, z.side + z.chunk :] = jnp.zeros((z.fields, z.edge - z.chunk), jnp.float32)


def message_kernel(z, tile_ref, state_ref, *message_refs):
    state = [state_ref[f] for f in range(z.fields)]
    write_messages(z, tile_ref[0], state, message_refs)


def scatter(z, table, pick_ref, place_ref, spread_ref):
    high, low = split(table)
    both = jnp.dot(
        jnp.concatenate([high, low], axis=0), pick_ref[...], preferred_element_type=jnp.float32
    )
    picked = both[: z.fields] + both[z.fields :]
    spread = [spread_ref[0], spread_ref[1]]
    left = jnp.concatenate(
        [picked[f : f + 1, :] * spread[b] for b in range(2) for f in range(z.fields)], axis=0
    )
    high, low = split(left)
    half = z.fields * z.rows
    product = jnp.dot(
        jnp.concatenate([high, low], axis=0), place_ref[...], preferred_element_type=jnp.float32
    )
    product = product[: 2 * half] + product[2 * half :]
    added = product[:half] + pltpu.roll(product[half:], 1, 1)
    return [added[f * z.rows : (f + 1) * z.rows] for f in range(z.fields)]


def border_mask(z, tile):
    row = lax.broadcasted_iota(jnp.int32, (z.rows, z.columns), 0)
    column = lax.broadcasted_iota(jnp.int32, (z.rows, z.columns), 1)
    return (
        ((row == 0) & (tile == 0))
        | ((row == z.rows - 1) & (tile == z.tiles - 1))
        | (column == 0)
        | (column == z.columns - 1)
    )


def overset_kernel(z, tile_ref, state_ref, pick_ref, place_ref, spread_ref, *refs):
    messages, (out_ref, table_ref, first_ref, last_ref) = refs[: z.tiles], refs[z.tiles :]
    tile = tile_ref[0]
    sides = messages[0][:, 0 : z.side]
    first = jnp.zeros((z.fields, z.edge), jnp.float32)
    last = first
    for k, ref in enumerate(messages):
        if k:
            sides = sides + ref[:, 0 : z.side]
        edge = ref[:, z.side :]
        first = jnp.where(tile == k, edge, first)
        last = jnp.where(lax.rem(tile + 1, z.tiles) == k, edge, last)
    table = jnp.concatenate([sides, first, last], axis=1)
    table_ref[...] = table
    added = scatter(z, table, pick_ref, place_ref, spread_ref)
    border = border_mask(z, tile)
    for f in range(z.fields):
        value = jnp.where(border, 0.0, state_ref[f]) + added[f]
        out_ref[f] = value
        first_ref[f : f + 1, :] = value[0:1, :]
        last_ref[f : f + 1, :] = value[z.rows - 1 : z.rows, :]


def operator_kernel(
    z,
    final,
    tile_ref,
    radial_ref,
    coupling_ref,
    radial_column_ref,
    kept_ref,
    below_row_ref,
    above_row_ref,
    level_below_ref,
    level_above_ref,
    table_below_ref,
    table_above_ref,
    pick_ref,
    place_ref,
    spread_ref,
    diffuse_ref,
    theta_ref,
    phi_ref,
    *refs,
):
    tile = tile_ref[0]
    border = border_mask(z, tile)
    row = lax.broadcasted_iota(jnp.int32, (z.rows, z.columns), 0)
    column = lax.broadcasted_iota(jnp.int32, (z.rows, z.columns), 1)
    table = (
        radial_column_ref[:, 0:1] * table_below_ref[...]
        + radial_column_ref[:, 1:2] * table_above_ref[...]
    )
    added = scatter(z, table, pick_ref, place_ref, spread_ref)
    diffuse = diffuse_ref[...]
    theta = theta_ref[...]
    phi = phi_ref[...]
    north = diffuse + theta
    south = diffuse - theta
    east = jnp.where(column == z.columns - 1, 0.0, diffuse + phi)
    west = jnp.where(column == 0, 0.0, diffuse - phi)
    center = 4.0 * diffuse
    values = []
    for f in range(z.fields):
        v = kept_ref[f]
        before = jnp.where(row == 0, below_row_ref[f : f + 1, :], pltpu.roll(v, 1, 0))
        after = jnp.where(
            row == z.rows - 1, above_row_ref[f : f + 1, :], pltpu.roll(v, z.rows - 1, 0)
        )
        total = south * before + north * after - center * v
        total = total + west * pltpu.roll(v, 1, 1) + east * pltpu.roll(v, z.columns - 1, 1)
        other = radial_ref[1, f] * level_below_ref[f] + radial_ref[2, f] * level_above_ref[f]
        total = total + radial_ref[0, f] * v + (jnp.where(border, 0.0, other) + added[f])
        for e in range(z.fields):
            total = total + coupling_ref[e, f] * kept_ref[e]
        if final:
            first_ref, out_ref = refs
            out_ref[f] = first_ref[f] + v + (0.5 * STEP_SIZE) * total
        else:
            total = STEP_SIZE * total
            refs[0][f] = total
            values.append(total)
    if not final:
        write_messages(z, tile, values, refs[1:])


def body(
    final_cotangent,
    diffusivity,
    theta_velocity,
    phi_velocity,
    radial_stencil,
    field_coupling,
    slot_targets,
    slot_donors,
    slot_weights,
    slot_counts,
):
    fields, levels, rows, columns = final_cotangent.shape[1:]
    tiles = lax.axis_size("hor")
    level_count = lax.axis_size("rad")
    z = Sizes(fields, rows, columns, tiles, slot_targets.shape[-1])
    tile = lax.axis_index("hor")
    level = lax.axis_index("rad")
    tile_array = tile[None].astype(jnp.int32)
    f32 = jnp.float32

    def call(kernel, outs, in_specs):
        return pl.pallas_call(
            kernel,
            out_shape=tuple(jax.ShapeDtypeStruct(shape, dtype) for shape, dtype in outs),
            in_specs=in_specs,
            out_specs=tuple(VMEM for _ in outs),
        )

    level_up = [(i, i + 1) for i in range(level_count - 1)]
    level_down = [(i + 1, i) for i in range(level_count - 1)]
    tile_up = [(i, i + 1) for i in range(tiles - 1)]
    tile_down = [(i + 1, i) for i in range(tiles - 1)]

    def neighbours(x, axis, up, down):
        return lax.ppermute(x, axis, up), lax.ppermute(x, axis, down)

    def exchange(messages):
        if tiles <= 8:
            return [
                lax.ppermute(
                    m,
                    ("panel", "hor"),
                    [
                        (p * tiles + t, (1 - p) * tiles + (t + k) % tiles)
                        for p in range(2)
                        for t in range(tiles)
                    ],
                )
                for k, m in enumerate(messages)
            ]
        places = jnp.arange(tiles, dtype=jnp.int32)
        stacked = jnp.stack(messages)[(places - tile) % tiles]
        stacked = lax.all_to_all(stacked, "hor", 0, 0, tiled=True)
        stacked = lax.ppermute(stacked, "panel", [(0, 1), (1, 0)])[(tile - places) % tiles]
        return [stacked[k] for k in range(tiles)]

    target = slot_targets[0, 0].reshape(z.groups, 4)[:, 0]
    donors = slot_donors[0, 0].reshape(z.groups, 4)
    weights = slot_weights[0, 0]
    weights = jnp.where(
        jnp.arange(weights.shape[0], dtype=jnp.int32) < slot_counts[0, 0], weights, f32(0.0)
    ).reshape(z.groups, 4)
    base = jnp.min(donors, axis=1)
    base_column = base % columns
    code = 2 * (donors // columns) + (donors % columns - base_column[:, None])
    total_rows = rows * tiles
    along = target - 2 * columns
    side, side_row = along // total_rows, along % total_rows
    place = (tile - side_row // rows) % tiles
    local = jnp.where(
        target < columns,
        z.side + target - tile * z.chunk,
        jnp.where(
            target < 2 * columns,
            z.side + z.edge + target - columns - tile * z.chunk,
            2 * rows * place + side * rows + side_row % rows,
        ),
    )
    pad = z.padded - z.groups
    local_row = jnp.pad(local, (0, pad), constant_values=-1)[None, :]
    code_rows = jnp.pad(code.T, ((0, 0), (0, pad)), constant_values=-1)
    weight_rows = jnp.pad(weights.T, ((0, 0), (0, pad)))
    column_column = jnp.pad(base_column, (0, pad), constant_values=-1)[:, None]
    maps = call(
        functools.partial(prepare_kernel, z),
        [
            ((z.table, z.padded), jnp.bfloat16),
            ((z.padded, columns), jnp.bfloat16),
            ((2, rows, z.padded), f32),
        ],
        [VMEM] * 4,
    )(local_row, code_rows, weight_rows, column_column)

    padded_stencil = jnp.pad(radial_stencil, ((0, 0), (0, 0), (1, 1)))
    radial = jnp.stack(
        [
            lax.dynamic_index_in_dim(padded_stencil[0], level + 1, 1, False),
            lax.dynamic_index_in_dim(padded_stencil[1], level, 1, False),
            lax.dynamic_index_in_dim(padded_stencil[2], level + 2, 1, False),
        ]
    )
    radial_columns = radial[1:].T
    coupling = lax.dynamic_index_in_dim(field_coupling, level, 0, False)
    coefficients = (diffusivity[0, 0], theta_velocity[0, 0], phi_velocity[0, 0])

    block = ((fields, rows, columns), f32)
    line = ((fields, columns), f32)
    message = ((fields, z.message), f32)

    def substep(state, messages, final, extra):
        level_below, level_above = neighbours(state, "rad", level_up, level_down)
        received = exchange(messages)
        kept, table, first, last = call(
            functools.partial(overset_kernel, z),
            [block, ((fields, z.table), f32), line, line],
            [SMEM] + [VMEM] * (4 + tiles),
        )(tile_array, state, *maps, *received)
        below_row = lax.ppermute(last, "hor", tile_up)
        above_row = lax.ppermute(first, "hor", tile_down)
        table_below, table_above = neighbours(table, "rad", level_up, level_down)
        outs = [block] if final else [block] + [message] * tiles
        results = call(
            functools.partial(operator_kernel, z, final),
            outs,
            [SMEM] * 3 + [VMEM] * (14 + len(extra)),
        )(
            tile_array,
            radial,
            coupling,
            radial_columns,
            kept,
            below_row,
            above_row,
            level_below,
            level_above,
            table_below,
            table_above,
            *maps,
            *coefficients,
            *extra,
        )
        return kept, results

    state = final_cotangent.reshape(fields, rows, columns)
    messages = call(
        functools.partial(message_kernel, z), [message] * tiles, [SMEM, VMEM]
    )(tile_array, state)
    after_full, results = substep(state, messages, False, ())
    pulled, messages = results[0], results[1:]
    _, results = substep(pulled, messages, True, (after_full,))
    return results[0].reshape(final_cotangent.shape)


def solution(mesh):
    return jax.shard_map(
        body,
        mesh=mesh,
        in_specs=(
            P("panel", None, "rad", "hor", None),
            P("panel", "rad", "hor", None),
            P("panel", "rad", "hor", None),
            P("panel", "rad", "hor", None),
            P(),
            P(),
            P("panel", "hor", None),
            P("panel", "hor", None),
            P("panel", "hor", None),
            P("panel", "hor"),
        ),
        out_specs=P("panel", None, "rad", "hor", None),
        check_vma=False,
    )
```

```python
import functools

import jax
import jax.numpy as jnp
from jax import lax
from jax.experimental import pallas as pl
from jax.experimental.pallas import tpu as pltpu
from jax.sharding import PartitionSpec as P

STEP_SIZE = 0.2
LANES = 128
VMEM = pl.BlockSpec(memory_space=pltpu.VMEM)
SMEM = pl.BlockSpec(memory_space=pltpu.SMEM)


def round_up(n, m):
    return -(-n // m) * m


class Sizes:
    def __init__(self, fields, rows, columns, tiles, levels, slots):
        self.fields, self.rows, self.columns, self.tiles = fields, rows, columns, tiles
        self.levels = levels
        self.chunk = columns // tiles
        self.edge = round_up(self.chunk, LANES)
        self.side = round_up(2 * rows * tiles, LANES)
        self.message = self.side + self.edge
        self.table = self.side + 2 * self.edge
        self.slots = slots
        self.groups = slots // 4
        self.padded = round_up(self.groups, LANES)


def split(x):
    high = x.astype(jnp.bfloat16)
    low = (x - high.astype(jnp.float32)).astype(jnp.bfloat16)
    return high, low


def pieces(x, count):
    out = []
    for _ in range(count):
        out.append(x.astype(jnp.bfloat16).astype(jnp.float32))
        x = x - out[-1]
    return out


def write_hits(z, index, out_ref):
    bf16 = jnp.bfloat16
    high = index >> 7
    low = index - (high << 7)
    own = lax.broadcasted_iota(jnp.int32, (LANES, LANES), 0).astype(bf16)
    one, zero = jnp.ones((LANES, LANES), bf16), jnp.zeros((LANES, LANES), bf16)
    for i in range(0, out_ref.shape[0], LANES):
        inside = jnp.where(high == i // LANES, low, -1).astype(bf16)
        for j in range(0, z.padded, LANES):
            hit = own == inside[:, j : j + LANES]
            out_ref[i : i + LANES, j : j + LANES] = jnp.where(hit, one, zero)


def prepare_kernel(z, *refs):
    hbm, (pick_ref, place_ref, spread_ref), (*held, sems) = refs[:4], refs[4:7], refs[7:]
    copies = [
        pltpu.make_async_copy(source, target, sems.at[i])
        for i, (source, target) in enumerate(zip(hbm, held))
    ]
    for copy in copies:
        copy.start()
    for copy in copies:
        copy.wait()
    count_ref, target_ref, donor_ref, weight_ref = held
    f32 = jnp.float32
    tile = lax.axis_index("hor")
    slot = lax.broadcasted_iota(jnp.int32, (1, z.slots), 1)
    weight = jnp.where(slot < count_ref[0, 0], weight_ref[...], 0.0)
    lists = pieces(target_ref[...].astype(f32), 2)
    lists += pieces(donor_ref[...].astype(f32), 2) + pieces(weight, 3)
    lists = jnp.concatenate(lists + [jnp.zeros((1, z.slots), f32)], axis=0)
    blocks = -(-z.slots // 256)
    if blocks * 256 > z.slots:
        tail = jnp.zeros((8, blocks * 256 - z.slots), f32)
        lists = jnp.concatenate([lists, tail], axis=1)
    stacked = jnp.concatenate([lists[:, 256 * b : 256 * (b + 1)] for b in range(blocks)], axis=0)
    lane_in = lax.broadcasted_iota(jnp.int32, (256, 256), 0)
    lane_out = lax.broadcasted_iota(jnp.int32, (256, 256), 1)
    move = jnp.where(lane_out == 64 * (lane_in & 3) + (lane_in >> 2), 1.0, 0.0)
    moved = jnp.dot(
        stacked.astype(jnp.bfloat16), move.astype(jnp.bfloat16), preferred_element_type=f32
    )
    quarter = []
    for q in range(4):
        parts = [moved[8 * b : 8 * (b + 1), 64 * q : 64 * (q + 1)] for b in range(blocks)]
        if z.padded > 64 * blocks:
            parts.append(jnp.zeros((8, z.padded - 64 * blocks), f32))
        quarter.append(jnp.concatenate(parts, axis=1)[:, : z.padded])
    group = lax.broadcasted_iota(jnp.int32, (1, z.padded), 1)
    target = quarter[0][0:1] + quarter[0][1:2]
    donors = [x[2:3] + x[3:4] for x in quarter]
    weights = [x[4:5] + x[5:6] + x[6:7] for x in quarter]

    def row_of(cell):
        row = jnp.zeros_like(cell)
        for i in range(1, z.rows):
            row = row + jnp.where(cell >= float(i * z.columns), 1.0, 0.0)
        return row

    base = jnp.minimum(jnp.minimum(donors[0], donors[1]), jnp.minimum(donors[2], donors[3]))
    base_column = base - row_of(base) * z.columns
    base_column = jnp.where(group < z.groups, base_column, -1.0).astype(jnp.int32)
    target = target.astype(jnp.int32)
    total_rows = z.rows * z.tiles
    along = target - 2 * z.columns
    side = jnp.where(along >= total_rows, 1, 0)
    side_row = along - total_rows * side
    owner = jnp.floor((side_row.astype(f32) + 0.5) * (1.0 / z.rows)).astype(jnp.int32)
    turn = tile - owner
    turn = turn + jnp.where(turn < 0, z.tiles, 0)
    side_place = 2 * z.rows * turn + z.rows * (side - owner) + side_row
    edge_place = z.side + target - tile * z.chunk
    local = jnp.where(
        target < z.columns,
        edge_place,
        jnp.where(target < 2 * z.columns, edge_place + z.edge - z.columns, side_place),
    )
    local = jnp.where(group < z.groups, local, -1)
    write_hits(z, local, pick_ref)
    write_hits(z, base_column, place_ref)
    rows = lax.broadcasted_iota(jnp.int32, (z.rows, z.padded), 0)
    for b in range(2):
        total = jnp.zeros((z.rows, z.padded), f32)
        for donor, weight in zip(donors, weights):
            row = row_of(donor)
            column = donor.astype(jnp.int32) - row.astype(jnp.int32) * z.columns
            hit = (rows == row.astype(jnp.int32)) & (column == base_column + b)
            total = total + jnp.where(hit, weight, 0.0)
        spread_ref[b] = total


def write_messages(z, tile, state, message_refs):
    first = jnp.concatenate([state[f][0:1, :] for f in range(z.fields)], axis=0)
    last = jnp.concatenate([state[f][z.rows - 1 : z.rows, :] for f in range(z.fields)], axis=0)
    edge = jnp.where(tile == z.tiles - 1, last, first)
    shift = lax.rem(z.columns - tile * z.chunk, z.columns)
    edge = pltpu.roll(edge, shift, 1)
    lane = lax.broadcasted_iota(jnp.int32, (z.rows, LANES), 1)
    row = lax.broadcasted_iota(jnp.int32, (z.rows, LANES), 0)
    sides = []
    for f in range(z.fields):
        left = jnp.where(lane == row, state[f][:, 0:1], 0.0)
        right = jnp.where(lane == row + z.rows, state[f][:, z.columns - 1 : z.columns], 0.0)
        sides.append(jnp.sum(left + right, axis=0, keepdims=True))
    sides = jnp.concatenate(sides, axis=0)
    if z.side > LANES:
        sides = jnp.concatenate([sides, jnp.zeros((z.fields, z.side - LANES), jnp.float32)], axis=1)
    for k, ref in enumerate(message_refs):
        ref[:, 0 : z.side] = pltpu.roll(sides, 2 * z.rows * k, 1) if k else sides
        ref[:, z.side : z.side + z.chunk] = edge[:, k * z.chunk : (k + 1) * z.chunk]
        if z.chunk < z.edge:
            ref[:, z.side + z.chunk :] = jnp.zeros((z.fields, z.edge - z.chunk), jnp.float32)


def message_kernel(z, state_ref, *message_refs):
    tile = lax.axis_index("hor")
    state = [state_ref[f] for f in range(z.fields)]
    write_messages(z, tile, state, message_refs)


def scatter(z, table, pick_ref, place_ref, spread_ref):
    high, low = split(table)
    both = jnp.dot(
        jnp.concatenate([high, low], axis=0), pick_ref[...], preferred_element_type=jnp.float32
    )
    picked = both[: z.fields] + both[z.fields :]
    spread = [spread_ref[0], spread_ref[1]]
    left = jnp.concatenate(
        [picked[f : f + 1, :] * spread[b] for b in range(2) for f in range(z.fields)], axis=0
    )
    high, low = split(left)
    half = z.fields * z.rows
    product = lax.dot_general(
        jnp.concatenate([high, low], axis=0),
        place_ref[...],
        (((1,), (1,)), ((), ())),
        preferred_element_type=jnp.float32,
    )
    product = product[: 2 * half] + product[2 * half :]
    added = product[:half] + pltpu.roll(product[half:], 1, 1)
    return [added[f * z.rows : (f + 1) * z.rows] for f in range(z.fields)]


def border_mask(z, tile):
    row = lax.broadcasted_iota(jnp.int32, (z.rows, z.columns), 0)
    column = lax.broadcasted_iota(jnp.int32, (z.rows, z.columns), 1)
    return (
        ((row == 0) & (tile == 0))
        | ((row == z.rows - 1) & (tile == z.tiles - 1))
        | (column == 0)
        | (column == z.columns - 1)
    )


def overset_kernel(z, state_ref, pick_ref, place_ref, spread_ref, *refs):
    messages, (out_ref, first_ref, last_ref) = refs[: z.tiles], refs[z.tiles :]
    tile = lax.axis_index("hor")
    sides = messages[0][:, 0 : z.side]
    first = jnp.zeros((z.fields, z.edge), jnp.float32)
    last = first
    for k, ref in enumerate(messages):
        if k:
            sides = sides + ref[:, 0 : z.side]
        edge = ref[:, z.side :]
        first = jnp.where(tile == k, edge, first)
        last = jnp.where(lax.rem(tile + 1, z.tiles) == k, edge, last)
    table = jnp.concatenate([sides, first, last], axis=1)
    added = scatter(z, table, pick_ref, place_ref, spread_ref)
    border = border_mask(z, tile)
    for f in range(z.fields):
        value = jnp.where(border, 0.0, state_ref[f]) + added[f]
        out_ref[f] = value
        first_ref[f : f + 1, :] = value[0:1, :]
        last_ref[f : f + 1, :] = value[z.rows - 1 : z.rows, :]


def operator_kernel(
    z,
    final,
    radial_ref,
    coupling_ref,
    state_ref,
    below_row_ref,
    above_row_ref,
    level_below_ref,
    level_above_ref,
    diffuse_ref,
    theta_ref,
    phi_ref,
    *refs,
):
    tile = lax.axis_index("hor")
    level = lax.axis_index("rad")
    below = jnp.maximum(level - 1, 0)
    above = jnp.minimum(level + 1, z.levels - 1)
    row = lax.broadcasted_iota(jnp.int32, (z.rows, z.columns), 0)
    column = lax.broadcasted_iota(jnp.int32, (z.rows, z.columns), 1)
    diffuse = diffuse_ref[...]
    theta = theta_ref[...]
    phi = phi_ref[...]
    north = diffuse + theta
    south = diffuse - theta
    east = jnp.where(column == z.columns - 1, 0.0, diffuse + phi)
    west = jnp.where(column == 0, 0.0, diffuse - phi)
    center = 4.0 * diffuse
    values = []
    for f in range(z.fields):
        v = state_ref[f]
        before = jnp.where(row == 0, below_row_ref[f : f + 1, :], pltpu.roll(v, 1, 0))
        after = jnp.where(
            row == z.rows - 1, above_row_ref[f : f + 1, :], pltpu.roll(v, z.rows - 1, 0)
        )
        total = south * before + north * after - center * v
        total = total + west * pltpu.roll(v, 1, 1) + east * pltpu.roll(v, z.columns - 1, 1)
        total = total + radial_ref[0, level, f] * v
        total = total + radial_ref[1, below, f] * level_below_ref[f]
        total = total + radial_ref[2, above, f] * level_above_ref[f]
        for e in range(z.fields):
            total = total + coupling_ref[level, e, f] * state_ref[e]
        if final:
            first_ref, out_ref = refs
            out_ref[f] = first_ref[f] + v + (0.5 * STEP_SIZE) * total
        else:
            total = STEP_SIZE * total
            refs[0][f] = total
            values.append(total)
    if not final:
        write_messages(z, tile, values, refs[1:])


def body(
    final_cotangent,
    diffusivity,
    theta_velocity,
    phi_velocity,
    radial_stencil,
    field_coupling,
    slot_targets,
    slot_donors,
    slot_weights,
    slot_counts,
):
    fields, levels, rows, columns = final_cotangent.shape[1:]
    tiles = lax.axis_size("hor")
    level_count = lax.axis_size("rad")
    z = Sizes(fields, rows, columns, tiles, level_count, slot_targets.shape[-1])
    tile = lax.axis_index("hor")
    f32 = jnp.float32

    def call(kernel, outs, in_specs, limit, scratch=()):
        return pl.pallas_call(
            kernel,
            out_shape=tuple(jax.ShapeDtypeStruct(shape, dtype) for shape, dtype in outs),
            in_specs=in_specs,
            out_specs=tuple(VMEM for _ in outs),
            scratch_shapes=scratch,
            compiler_params=pltpu.CompilerParams(vmem_limit_bytes=limit << 20),
        )

    level_up = [(i, i + 1) for i in range(level_count - 1)]
    level_down = [(i + 1, i) for i in range(level_count - 1)]
    tile_up = [(i, i + 1) for i in range(tiles - 1)]
    tile_down = [(i + 1, i) for i in range(tiles - 1)]

    def exchange(messages):
        if tiles <= 8:
            return [
                lax.ppermute(
                    m,
                    ("panel", "hor"),
                    [
                        (p * tiles + t, (1 - p) * tiles + (t + k) % tiles)
                        for p in range(2)
                        for t in range(tiles)
                    ],
                )
                for k, m in enumerate(messages)
            ]
        places = jnp.arange(tiles, dtype=jnp.int32)
        stacked = jnp.stack(messages)[(places - tile) % tiles]
        stacked = lax.all_to_all(stacked, "hor", 0, 0, tiled=True)
        stacked = lax.ppermute(stacked, "panel", [(0, 1), (1, 0)])[(tile - places) % tiles]
        return [stacked[k] for k in range(tiles)]

    maps = call(
        functools.partial(prepare_kernel, z),
        [
            ((z.table, z.padded), jnp.bfloat16),
            ((columns, z.padded), jnp.bfloat16),
            ((2, rows, z.padded), f32),
        ],
        [pl.BlockSpec(memory_space=pl.ANY)] * 4,
        12,
        (
            pltpu.SMEM((1, 1), jnp.int32),
            pltpu.VMEM((1, z.slots), jnp.int32),
            pltpu.VMEM((1, z.slots), jnp.int32),
            pltpu.VMEM((1, z.slots), f32),
            pltpu.SemaphoreType.DMA((4,)),
        ),
    )(slot_counts, slot_targets[0], slot_donors[0], slot_weights[0])
    coefficients = (diffusivity[0, 0], theta_velocity[0, 0], phi_velocity[0, 0])

    block = ((fields, rows, columns), f32)
    line = ((fields, columns), f32)
    message = ((fields, z.message), f32)

    def substep(state, messages, final, extra):
        received = exchange(messages)
        full, first, last = call(
            functools.partial(overset_kernel, z), [block, line, line], [VMEM] * (4 + tiles), 8
        )(state, *maps, *received)
        level_below = lax.ppermute(full, "rad", level_up)
        level_above = lax.ppermute(full, "rad", level_down)
        below_row = lax.ppermute(last, "hor", tile_up)
        above_row = lax.ppermute(first, "hor", tile_down)
        outs = [block] if final else [block] + [message] * tiles
        results = call(
            functools.partial(operator_kernel, z, final),
            outs,
            [SMEM] * 2 + [VMEM] * (8 + len(extra)),
            8,
        )(
            jnp.transpose(radial_stencil, (0, 2, 1)),
            field_coupling,
            full,
            below_row,
            above_row,
            level_below,
            level_above,
            *coefficients,
            *extra,
        )
        return full, results

    state = final_cotangent.reshape(fields, rows, columns)
    messages = call(functools.partial(message_kernel, z), [message] * tiles, [VMEM], 4)(state)
    after_full, results = substep(state, messages, False, ())
    pulled, messages = results[0], results[1:]
    _, results = substep(pulled, messages, True, (after_full,))
    return results[0].reshape(final_cotangent.shape)


def solution(mesh):
    return jax.shard_map(
        body,
        mesh=mesh,
        in_specs=(
            P("panel", None, "rad", "hor", None),
            P("panel", "rad", "hor", None),
            P("panel", "rad", "hor", None),
            P("panel", "rad", "hor", None),
            P(),
            P(),
            P("panel", "hor", None),
            P("panel", "hor", None),
            P("panel", "hor", None),
            P("panel", "hor"),
        ),
        out_specs=P("panel", None, "rad", "hor", None),
        check_vma=False,
    )
```

```python
import functools

import jax
import jax.numpy as jnp
from jax import lax
from jax.experimental import pallas as pl
from jax.experimental.pallas import tpu as pltpu
from jax.sharding import PartitionSpec as P

STEP_SIZE = 0.2
LANES = 128
VMEM = pl.BlockSpec(memory_space=pltpu.VMEM)
HBM = pl.BlockSpec(memory_space=pltpu.HBM)
SMEM = pl.BlockSpec(memory_space=pltpu.SMEM)


def round_up(n, m):
    return -(-n // m) * m


class Sizes:
    def __init__(self, fields, rows, columns, tiles, levels, slots):
        self.fields, self.rows, self.columns, self.tiles = fields, rows, columns, tiles
        self.levels = levels
        self.chunk = columns // tiles
        self.edge = round_up(self.chunk, LANES)
        self.message = round_up(self.chunk + 2 * rows * tiles, LANES)
        self.table = self.message + self.edge
        self.paired = tiles & (tiles - 1) == 0
        self.order = list(reversed(range(tiles)))
        self.slots = slots
        self.groups = slots // 4
        self.padded = round_up(self.groups, LANES)


    def target(self, source, k):
        return source ^ k if self.paired else (source + k) % self.tiles

    def source(self, target, k):
        return target ^ k if self.paired else (target - k) % self.tiles

    def turn(self, source, target):
        return source ^ target if self.paired else (target - source) % self.tiles


def split(x):
    high = x.astype(jnp.bfloat16)
    low = (x - high.astype(jnp.float32)).astype(jnp.bfloat16)
    return high, low


def pieces(x, count):
    out = []
    for _ in range(count):
        out.append(x.astype(jnp.bfloat16).astype(jnp.float32))
        x = x - out[-1]
    return out


def write_hits(z, index, out_ref):
    bf16 = jnp.bfloat16
    high = index >> 7
    low = index - (high << 7)
    own = lax.broadcasted_iota(jnp.int32, (LANES, LANES), 0).astype(bf16)
    one, zero = jnp.ones((LANES, LANES), bf16), jnp.zeros((LANES, LANES), bf16)
    for i in range(0, out_ref.shape[0], LANES):
        inside = jnp.where(high == i // LANES, low, -1).astype(bf16)
        for j in range(0, z.padded, LANES):
            hit = own == inside[:, j : j + LANES]
            out_ref[i : i + LANES, j : j + LANES] = jnp.where(hit, one, zero)


def prepare_kernel(z, *refs):
    count_ref, target_ref, donor_ref, weight_ref, state_ref = refs[:5]
    pick_ref, place_ref, spread_ref, held_ref, sem = refs[5:]
    copy = pltpu.make_async_copy(state_ref, held_ref, sem)
    copy.start()
    f32 = jnp.float32
    slot = lax.broadcasted_iota(jnp.int32, (1, z.slots), 1)
    weight = jnp.where(slot < count_ref[0, 0], weight_ref[...], 0.0)
    tile = lax.axis_index("hor")
    lists = pieces(target_ref[...].astype(f32), 2)
    lists += pieces(donor_ref[...].astype(f32), 2) + pieces(weight, 3)
    lists = jnp.concatenate(lists + [jnp.zeros((1, z.slots), f32)], axis=0)
    blocks = -(-z.slots // 256)
    if blocks * 256 > z.slots:
        tail = jnp.zeros((8, blocks * 256 - z.slots), f32)
        lists = jnp.concatenate([lists, tail], axis=1)
    stacked = jnp.concatenate([lists[:, 256 * b : 256 * (b + 1)] for b in range(blocks)], axis=0)
    lane_in = lax.broadcasted_iota(jnp.int32, (256, 256), 0)
    lane_out = lax.broadcasted_iota(jnp.int32, (256, 256), 1)
    move = jnp.where(lane_out == 64 * (lane_in & 3) + (lane_in >> 2), 1.0, 0.0)
    moved = jnp.dot(
        stacked.astype(jnp.bfloat16), move.astype(jnp.bfloat16), preferred_element_type=f32
    )
    quarter = []
    for q in range(4):
        parts = [moved[8 * b : 8 * (b + 1), 64 * q : 64 * (q + 1)] for b in range(blocks)]
        if z.padded > 64 * blocks:
            parts.append(jnp.zeros((8, z.padded - 64 * blocks), f32))
        quarter.append(jnp.concatenate(parts, axis=1)[:, : z.padded])
    group = lax.broadcasted_iota(jnp.int32, (1, z.padded), 1)
    target = quarter[0][0:1] + quarter[0][1:2]
    donors = [x[2:3] + x[3:4] for x in quarter]
    weights = [x[4:5] + x[5:6] + x[6:7] for x in quarter]

    def row_of(cell):
        row = jnp.zeros_like(cell)
        for i in range(1, z.rows):
            row = row + jnp.where(cell >= float(i * z.columns), 1.0, 0.0)
        return row

    base = jnp.minimum(jnp.minimum(donors[0], donors[1]), jnp.minimum(donors[2], donors[3]))
    base_column = base - row_of(base) * z.columns
    base_column = jnp.where(group < z.groups, base_column, -1.0).astype(jnp.int32)
    target = target.astype(jnp.int32)
    total_rows = z.rows * z.tiles
    along = target - 2 * z.columns
    side = jnp.where(along >= total_rows, 1, 0)
    side_row = along - total_rows * side
    owner = jnp.floor((side_row.astype(f32) + 0.5) * (1.0 / z.rows)).astype(jnp.int32)
    if z.paired:
        turn = jnp.full_like(owner, tile) ^ owner
    else:
        turn = tile - owner + jnp.where(owner > tile, z.tiles, 0)
    side_place = z.chunk + 2 * z.rows * turn + z.rows * (side - owner) + side_row
    edge_place = target - tile * z.chunk
    local = jnp.where(
        target < z.columns,
        edge_place,
        jnp.where(target < 2 * z.columns, edge_place + z.message - z.columns, side_place),
    )
    local = jnp.where(group < z.groups, local, -1)
    write_hits(z, local, pick_ref)
    write_hits(z, base_column, place_ref)
    rows = lax.broadcasted_iota(jnp.int32, (z.rows, z.padded), 0)
    for b in range(2):
        total = jnp.zeros((z.rows, z.padded), f32)
        for donor, weight in zip(donors, weights):
            row = row_of(donor)
            column = donor.astype(jnp.int32) - row.astype(jnp.int32) * z.columns
            hit = (rows == row.astype(jnp.int32)) & (column == base_column + b)
            total = total + jnp.where(hit, weight, 0.0)
        spread_ref[b] = total
    copy.wait()


def write_messages(z, tile, edge, left, right, message_refs):
    lane = lax.broadcasted_iota(jnp.int32, (z.rows, LANES), 1)
    row = lax.broadcasted_iota(jnp.int32, (z.rows, LANES), 0)
    sides = []
    for f in range(z.fields):
        one = jnp.where(lane == row, left[f], 0.0)
        two = jnp.where(lane == row + z.rows, right[f], 0.0)
        sides.append(jnp.sum(one + two, axis=0, keepdims=True))
    sides = jnp.concatenate(sides, axis=0)
    sides = jnp.concatenate(
        [sides, jnp.zeros((z.fields, z.message - LANES), jnp.float32)], axis=1
    )
    inside = lax.broadcasted_iota(jnp.int32, (z.fields, z.message), 1) < z.chunk
    for k, ref in zip(z.order, message_refs):
        offset = z.target(tile, k) * z.chunk
        part = pltpu.roll(edge, lax.rem(z.columns - offset, z.columns), 1)[:, : z.message]
        ref[...] = jnp.where(inside, part, pltpu.roll(sides, z.chunk + 2 * z.rows * k, 1))


def start_kernel(z, state_ref, target_ref, donor_ref, weight_ref, *refs):
    messages, lists, (first_ref, last_ref, left_ref, right_ref, sems) = (
        refs[: z.tiles],
        refs[z.tiles : z.tiles + 3],
        refs[z.tiles + 3 :],
    )
    pairs = [
        (state_ref.at[:, pl.ds(0, 1), :], first_ref),
        (state_ref.at[:, pl.ds(z.rows - 1, 1), :], last_ref),
        (state_ref.at[:, :, pl.ds(0, LANES)], left_ref),
        (state_ref.at[:, :, pl.ds(z.columns - LANES, LANES)], right_ref),
        (target_ref, lists[0]),
        (donor_ref, lists[1]),
        (weight_ref, lists[2]),
    ]
    copies = [pltpu.make_async_copy(a, b, sems.at[i]) for i, (a, b) in enumerate(pairs)]
    for copy in copies:
        copy.start()
    tile = lax.axis_index("hor")
    for copy in copies:
        copy.wait()
    rows = [jnp.where(tile == z.tiles - 1, last_ref[f], first_ref[f]) for f in range(z.fields)]
    left = [left_ref[f][:, 0:1] for f in range(z.fields)]
    right = [right_ref[f][:, LANES - 1 : LANES] for f in range(z.fields)]
    write_messages(z, tile, jnp.concatenate(rows, axis=0), left, right, messages)


def scatter(z, table, pick_ref, place_ref, spread_ref):
    high, low = split(table)
    both = jnp.dot(
        jnp.concatenate([high, low], axis=0), pick_ref[...], preferred_element_type=jnp.float32
    )
    picked = both[: z.fields] + both[z.fields :]
    spread = [spread_ref[0], spread_ref[1]]
    left = jnp.concatenate(
        [picked[f : f + 1, :] * spread[b] for b in range(2) for f in range(z.fields)], axis=0
    )
    high, low = split(left)
    half = z.fields * z.rows
    product = lax.dot_general(
        jnp.concatenate([high, low], axis=0),
        place_ref[...],
        (((1,), (1,)), ((), ())),
        preferred_element_type=jnp.float32,
    )
    product = product[: 2 * half] + product[2 * half :]
    added = product[:half] + pltpu.roll(product[half:], 1, 1)
    return [added[f * z.rows : (f + 1) * z.rows] for f in range(z.fields)]


def border_mask(z, tile):
    row = lax.broadcasted_iota(jnp.int32, (z.rows, z.columns), 0)
    column = lax.broadcasted_iota(jnp.int32, (z.rows, z.columns), 1)
    return (
        ((row == 0) & (tile == 0))
        | ((row == z.rows - 1) & (tile == z.tiles - 1))
        | (column == 0)
        | (column == z.columns - 1)
    )


def overset_kernel(z, state_ref, pick_ref, place_ref, spread_ref, *refs):
    messages, (out_ref, ahead_ref, behind_ref) = refs[: z.tiles], refs[z.tiles :]
    tile = lax.axis_index("hor")
    inside = lax.broadcasted_iota(jnp.int32, (z.fields, z.message), 1) < z.chunk
    first = jnp.zeros((z.fields, z.message), jnp.float32)
    last = jnp.zeros((z.fields, z.edge), jnp.float32)
    for k, ref in zip(z.order, messages):
        message = ref[...]
        use = jnp.where(z.turn(0, tile) == k, 1, 0)
        first = first + jnp.where(inside & (use == 0), 0.0, message)
        last = jnp.where(z.turn(z.tiles - 1, tile) == k, message[:, : z.edge], last)
    table = jnp.concatenate([first, last], axis=1)
    added = scatter(z, table, pick_ref, place_ref, spread_ref)
    border = border_mask(z, tile)
    even = lax.rem(tile, 2) == 0
    for f in range(z.fields):
        value = jnp.where(border, 0.0, state_ref[f]) + added[f]
        out_ref[f] = value
        first_row, last_row = value[0:1, :], value[z.rows - 1 : z.rows, :]
        ahead_ref[f : f + 1, :] = jnp.where(even, last_row, first_row)
        behind_ref[f : f + 1, :] = jnp.where(even, first_row, last_row)


def local_kernel(
    z,
    final,
    radial_ref,
    coupling_ref,
    state_ref,
    row_one_ref,
    row_two_ref,
    diffuse_ref,
    theta_ref,
    phi_ref,
    *refs,
):
    tile = lax.axis_index("hor")
    level = lax.axis_index("rad")
    even = lax.rem(tile, 2) == 0
    row_one, row_two = row_one_ref[...], row_two_ref[...]
    below_row = jnp.where(tile > 0, jnp.where(even, row_two, row_one), 0.0)
    above_row = jnp.where(tile < z.tiles - 1, jnp.where(even, row_one, row_two), 0.0)
    row = lax.broadcasted_iota(jnp.int32, (z.rows, z.columns), 0)
    column = lax.broadcasted_iota(jnp.int32, (z.rows, z.columns), 1)
    diffuse = diffuse_ref[...]
    theta = theta_ref[...]
    phi = phi_ref[...]
    north = diffuse + theta
    south = diffuse - theta
    east = jnp.where(column == z.columns - 1, 0.0, diffuse + phi)
    west = jnp.where(column == 0, 0.0, diffuse - phi)
    center = 4.0 * diffuse
    out_ref = refs[-1]
    for f in range(z.fields):
        v = state_ref[f]
        before = jnp.where(row == 0, below_row[f : f + 1, :], pltpu.roll(v, 1, 0))
        after = jnp.where(
            row == z.rows - 1, above_row[f : f + 1, :], pltpu.roll(v, z.rows - 1, 0)
        )
        total = south * before + north * after + (radial_ref[0, level, f] - center) * v
        total = total + west * pltpu.roll(v, 1, 1) + east * pltpu.roll(v, z.columns - 1, 1)
        for e in range(z.fields):
            total = total + coupling_ref[level, e, f] * state_ref[e]
        if final:
            out_ref[f] = refs[0][f] + v + (0.5 * STEP_SIZE) * total
        else:
            out_ref[f] = STEP_SIZE * total


def finish_kernel(z, final, radial_ref, base_ref, one_ref, two_ref, out_ref, *message_refs):
    level = lax.axis_index("rad")
    below = jnp.maximum(level - 1, 0)
    above = jnp.minimum(level + 1, z.levels - 1)
    step = 0.5 * STEP_SIZE if final else STEP_SIZE
    from_below = jnp.where(level > 0, step, 0.0)
    from_above = jnp.where(level < z.levels - 1, step, 0.0)
    one_above = lax.rem(level + lax.axis_index("panel"), 2) == 0
    values = []
    for f in range(z.fields):
        upper = from_below * radial_ref[1, below, f]
        lower = from_above * radial_ref[2, above, f]
        total = base_ref[f] + jnp.where(one_above, lower, upper) * one_ref[f]
        total = total + jnp.where(one_above, upper, lower) * two_ref[f]
        out_ref[f] = total
        values.append(total)
    if not final:
        tile = lax.axis_index("hor")
        first = jnp.concatenate([v[0:1] for v in values], axis=0)
        last = jnp.concatenate([v[z.rows - 1 : z.rows] for v in values], axis=0)
        left = [v[:, 0:1] for v in values]
        right = [v[:, z.columns - 1 : z.columns] for v in values]
        edge = jnp.where(tile == z.tiles - 1, last, first)
        write_messages(z, tile, edge, left, right, message_refs)


def partners(count, odd):
    out = []
    for i in range(count):
        j = ((i + odd) ^ 1) - odd
        out.append(j if 0 <= j < count else i)
    return out


def body(
    final_cotangent,
    diffusivity,
    theta_velocity,
    phi_velocity,
    radial_stencil,
    field_coupling,
    slot_targets,
    slot_donors,
    slot_weights,
    slot_counts,
):
    fields, levels, rows, columns = final_cotangent.shape[1:]
    tiles = lax.axis_size("hor")
    z = Sizes(fields, rows, columns, tiles, lax.axis_size("rad"), slot_targets.shape[-1])
    tile = lax.axis_index("hor")
    f32 = jnp.float32

    def call(kernel, outs, in_specs, limit, scratch=()):
        return pl.pallas_call(
            kernel,
            out_shape=tuple(jax.ShapeDtypeStruct(shape, dtype) for shape, dtype in outs),
            in_specs=in_specs,
            out_specs=tuple(VMEM for _ in outs),
            scratch_shapes=scratch,
            compiler_params=pltpu.CompilerParams(vmem_limit_bytes=limit << 20),
        )

    def meet_levels(x):
        count = lax.axis_size("rad")
        found = []
        for turn in range(2):
            pairs = [
                (p * count + i, p * count + j)
                for p in range(2)
                for i, j in enumerate(partners(count, p ^ turn))
            ]
            found.append(lax.ppermute(x, ("panel", "rad"), pairs))
        return found

    def meet_rows(ahead, behind):
        return [
            lax.ppermute(x, "hor", list(enumerate(partners(tiles, odd))))
            for odd, x in enumerate((ahead, behind))
        ]

    def exchange(messages):
        if tiles <= 8:
            return [
                lax.ppermute(
                    m,
                    ("panel", "hor"),
                    [
                        (p * tiles + t, (1 - p) * tiles + z.target(t, k))
                        for p in range(2)
                        for t in range(tiles)
                    ],
                )
                for k, m in zip(z.order, messages)
            ]
        places = jnp.arange(tiles, dtype=jnp.int32)
        stacked = jnp.stack(messages)[tiles - 1 - z.turn(tile, places)]
        stacked = lax.all_to_all(stacked, "hor", 0, 0, tiled=True)
        stacked = lax.ppermute(stacked, "panel", [(0, 1), (1, 0)])[z.source(tile, places)]
        return [stacked[k] for k in z.order]

    radial = jnp.transpose(radial_stencil, (0, 2, 1))
    coefficients = (diffusivity[0, 0], theta_velocity[0, 0], phi_velocity[0, 0])

    block = ((fields, rows, columns), f32)
    line = ((fields, columns), f32)
    message = ((fields, z.message), f32)

    def substep(state, messages, maps, final, extra):
        received = exchange(messages)
        if maps is None:
            *maps, state = prepare(state)
        full, ahead, behind = call(
            functools.partial(overset_kernel, z), [block, line, line], [VMEM] * (4 + tiles), 8
        )(state, *maps, *received)
        levels = meet_levels(full)
        rows_met = meet_rows(ahead, behind)
        (base,) = call(
            functools.partial(local_kernel, z, final),
            [block],
            [SMEM] * 2 + [VMEM] * (6 + len(extra)),
            8,
        )(radial, field_coupling, full, *rows_met, *coefficients, *extra)
        results = call(
            functools.partial(finish_kernel, z, final),
            [block] if final else [block] + [message] * tiles,
            [SMEM] + [VMEM] * 3,
            4,
        )(radial, base, *levels)
        return full, results, maps

    def in_hbm(x):
        return pltpu.with_memory_space_constraint(x, pltpu.HBM)

    state = in_hbm(final_cotangent.reshape(fields, rows, columns))
    slot_line = (1, z.slots)
    row_piece = pltpu.VMEM((fields, 1, columns), f32)
    side_piece = pltpu.VMEM((fields, rows, LANES), f32)
    started = call(
        functools.partial(start_kernel, z),
        [message] * tiles + [(slot_line, jnp.int32), (slot_line, jnp.int32), (slot_line, f32)],
        [HBM] * 4,
        4,
        [row_piece, row_piece, side_piece, side_piece, pltpu.SemaphoreType.DMA((7,))],
    )(state, in_hbm(slot_targets[0]), in_hbm(slot_donors[0]), in_hbm(slot_weights[0]))
    messages, lists = started[:tiles], started[tiles:]

    def prepare(state):
        return call(
            functools.partial(prepare_kernel, z),
            [
                ((z.table, z.padded), jnp.bfloat16),
                ((columns, z.padded), jnp.bfloat16),
                ((2, rows, z.padded), f32),
                block,
            ],
            [SMEM] + [VMEM] * 3 + [HBM],
            12,
            [pltpu.SemaphoreType.DMA],
        )(slot_counts, *lists, state)

    after_full, results, maps = substep(state, messages, None, False, ())
    pulled, messages = results[0], results[1:]
    _, results, _ = substep(pulled, messages, maps, True, (after_full,))
    return results[0].reshape(final_cotangent.shape)


def solution(mesh):
    return jax.shard_map(
        body,
        mesh=mesh,
        in_specs=(
            P("panel", None, "rad", "hor", None),
            P("panel", "rad", "hor", None),
            P("panel", "rad", "hor", None),
            P("panel", "rad", "hor", None),
            P(),
            P(),
            P("panel", "hor", None),
            P("panel", "hor", None),
            P("panel", "hor", None),
            P("panel", "hor"),
        ),
        out_specs=P("panel", None, "rad", "hor", None),
        check_vma=False,
    )
```

```python
import functools

import jax
import jax.numpy as jnp
from jax import lax
from jax.experimental import pallas as pl
from jax.experimental.pallas import tpu as pltpu
from jax.sharding import PartitionSpec as P

STEP_SIZE = 0.2
LANES = 128
PERMUTED_TILES = 8
VMEM = pl.BlockSpec(memory_space=pltpu.VMEM)
HBM = pl.BlockSpec(memory_space=pltpu.HBM)
SMEM = pl.BlockSpec(memory_space=pltpu.SMEM)


def round_up(n, m):
    return -(-n // m) * m


class Sizes:
    def __init__(self, fields, rows, columns, tiles, levels, slots):
        self.fields, self.rows, self.columns, self.tiles = fields, rows, columns, tiles
        self.levels = levels
        self.chunk = columns // tiles
        self.edge = round_up(self.chunk, LANES)
        self.message = round_up(self.chunk + 2 * rows * tiles, LANES)
        self.table = self.message + self.edge
        self.paired = tiles & (tiles - 1) == 0
        self.constants = fields * (fields + 5)
        self.order = list(reversed(range(tiles)))
        self.slots = slots
        self.groups = slots // 4
        self.padded = round_up(self.groups, LANES)


    def factor(self, final, f, side):
        return self.fields * (self.fields + 1 + 2 * final) + 2 * f + side

    def target(self, source, k):
        return source ^ k if self.paired else (source + k) % self.tiles

    def source(self, target, k):
        return target ^ k if self.paired else (target - k) % self.tiles

    def turn(self, source, target):
        return source ^ target if self.paired else (target - source) % self.tiles


def split(x):
    high = x.astype(jnp.bfloat16)
    low = (x - high.astype(jnp.float32)).astype(jnp.bfloat16)
    return high, low


def pieces(x, count):
    out = []
    for _ in range(count):
        out.append(x.astype(jnp.bfloat16).astype(jnp.float32))
        x = x - out[-1]
    return out


def write_hits(z, index, out_ref):
    bf16 = jnp.bfloat16
    high = index >> 7
    low = index - (high << 7)
    own = lax.broadcasted_iota(jnp.int32, (LANES, LANES), 0).astype(bf16)
    one, zero = jnp.ones((LANES, LANES), bf16), jnp.zeros((LANES, LANES), bf16)
    for i in range(0, out_ref.shape[0], LANES):
        inside = jnp.where(high == i // LANES, low, -1).astype(bf16)
        for j in range(0, z.padded, LANES):
            hit = own == inside[:, j : j + LANES]
            out_ref[i : i + LANES, j : j + LANES] = jnp.where(hit, one, zero)


def write_constants(z, radial_ref, coupling_ref, constant_ref, column_ref):
    level = lax.axis_index("rad")
    below = jnp.maximum(level - 1, 0)
    above = jnp.minimum(level + 1, z.levels - 1)
    first_above = (lax.rem(level, 2) == 0, lax.rem(level + lax.axis_index("panel"), 2) == 0)
    row = lax.broadcasted_iota(jnp.int32, (z.fields, LANES), 0)
    columns = [jnp.zeros((z.fields, LANES), jnp.float32)] * 2

    def write(index, value):
        constant_ref[index] = jnp.full((z.rows, LANES), value, jnp.float32)

    for f in range(z.fields):
        for e in range(z.fields):
            write(e * z.fields + f, coupling_ref[level, e, f])
        write(z.fields * z.fields + f, radial_ref[0, level, f])
        upper = jnp.where(level > 0, radial_ref[1, below, f], 0.0)
        lower = jnp.where(level < z.levels - 1, radial_ref[2, above, f], 0.0)
        for final, above_first in enumerate(first_above):
            step = 0.5 * STEP_SIZE if final else STEP_SIZE
            factors = [
                step * jnp.where(above_first, lower, upper),
                step * jnp.where(above_first, upper, lower),
            ]
            for side, factor in enumerate(factors):
                write(z.factor(final, f, side), factor)
            if not final:
                columns = [jnp.where(row == f, a, b) for a, b in zip(factors, columns)]
    for side, column in enumerate(columns):
        column_ref[side] = column


def spread(constant, shape):
    return jnp.concatenate([constant[: shape[0]]] * (shape[1] // LANES), axis=1)


def finished(z, final, f, constant_ref, base, one, two):
    factors = [spread(constant_ref[z.factor(final, f, side)], base.shape) for side in range(2)]
    return base + factors[0] * one + factors[1] * two


def prepare_kernel(z, *refs):
    count_ref, target_ref, donor_ref, weight_ref = refs[:4]
    sources, (pick_ref, place_ref, spread_ref, held_ref, constant_ref, column_ref) = (
        refs[4:7],
        refs[7:13],
    )
    radial_ref, coupling_ref, sems = refs[13:]
    copies = [
        pltpu.make_async_copy(source, target, sems.at[i])
        for i, (source, target) in enumerate(zip(sources, (held_ref, radial_ref, coupling_ref)))
    ]
    for copy in copies:
        copy.start()
    f32 = jnp.float32
    slot = lax.broadcasted_iota(jnp.int32, (1, z.slots), 1)
    weight = jnp.where(slot < count_ref[0, 0], weight_ref[...], 0.0)
    tile = lax.axis_index("hor")
    lists = pieces(target_ref[...].astype(f32), 2)
    lists += pieces(donor_ref[...].astype(f32), 2) + pieces(weight, 3)
    lists = jnp.concatenate(lists + [jnp.zeros((1, z.slots), f32)], axis=0)
    blocks = -(-z.slots // 256)
    if blocks * 256 > z.slots:
        tail = jnp.zeros((8, blocks * 256 - z.slots), f32)
        lists = jnp.concatenate([lists, tail], axis=1)
    stacked = jnp.concatenate([lists[:, 256 * b : 256 * (b + 1)] for b in range(blocks)], axis=0)
    lane_in = lax.broadcasted_iota(jnp.int32, (256, 256), 0)
    lane_out = lax.broadcasted_iota(jnp.int32, (256, 256), 1)
    move = jnp.where(lane_out == 64 * (lane_in & 3) + (lane_in >> 2), 1.0, 0.0)
    moved = jnp.dot(
        stacked.astype(jnp.bfloat16), move.astype(jnp.bfloat16), preferred_element_type=f32
    )
    quarter = []
    for q in range(4):
        parts = [moved[8 * b : 8 * (b + 1), 64 * q : 64 * (q + 1)] for b in range(blocks)]
        if z.padded > 64 * blocks:
            parts.append(jnp.zeros((8, z.padded - 64 * blocks), f32))
        quarter.append(jnp.concatenate(parts, axis=1)[:, : z.padded])
    group = lax.broadcasted_iota(jnp.int32, (1, z.padded), 1)
    target = quarter[0][0:1] + quarter[0][1:2]
    donors = [x[2:3] + x[3:4] for x in quarter]
    weights = [x[4:5] + x[5:6] + x[6:7] for x in quarter]

    def row_of(cell):
        row = jnp.zeros_like(cell)
        for i in range(1, z.rows):
            row = row + jnp.where(cell >= float(i * z.columns), 1.0, 0.0)
        return row

    base = jnp.minimum(jnp.minimum(donors[0], donors[1]), jnp.minimum(donors[2], donors[3]))
    base_column = base - row_of(base) * z.columns
    base_column = jnp.where(group < z.groups, base_column, -1.0).astype(jnp.int32)
    target = target.astype(jnp.int32)
    total_rows = z.rows * z.tiles
    along = target - 2 * z.columns
    side = jnp.where(along >= total_rows, 1, 0)
    side_row = along - total_rows * side
    owner = jnp.floor((side_row.astype(f32) + 0.5) * (1.0 / z.rows)).astype(jnp.int32)
    if z.paired:
        turn = jnp.full_like(owner, tile) ^ owner
    else:
        turn = tile - owner + jnp.where(owner > tile, z.tiles, 0)
    side_place = z.chunk + 2 * z.rows * turn + z.rows * (side - owner) + side_row
    edge_place = target - tile * z.chunk
    local = jnp.where(
        target < z.columns,
        edge_place,
        jnp.where(target < 2 * z.columns, edge_place + z.message - z.columns, side_place),
    )
    local = jnp.where(group < z.groups, local, -1)
    high = local >> 7
    pick_ref[0] = jnp.broadcast_to(high, (z.fields, z.padded))
    pick_ref[1] = jnp.broadcast_to(local - (high << 7), (z.fields, z.padded))
    write_hits(z, base_column, place_ref)
    rows = lax.broadcasted_iota(jnp.int32, (z.rows, z.padded), 0)
    for b in range(2):
        total = jnp.zeros((z.rows, z.padded), f32)
        for donor, weight in zip(donors, weights):
            row = row_of(donor)
            column = donor.astype(jnp.int32) - row.astype(jnp.int32) * z.columns
            hit = (rows == row.astype(jnp.int32)) & (column == base_column + b)
            total = total + jnp.where(hit, weight, 0.0)
        spread_ref[b] = total
    for copy in copies:
        copy.wait()
    write_constants(z, radial_ref, coupling_ref, constant_ref, column_ref)


def border_piece(z, tile, first, last, left, right):
    lane = lax.broadcasted_iota(jnp.int32, (z.rows, LANES), 1)
    row = lax.broadcasted_iota(jnp.int32, (z.rows, LANES), 0)
    sides = []
    for f in range(z.fields):
        one = jnp.where(lane == row, left[f], 0.0)
        two = jnp.where(lane == row + z.rows, right[f], 0.0)
        sides.append(jnp.sum(one + two, axis=0, keepdims=True))
    edge = jnp.where(
        tile == z.tiles - 1, jnp.concatenate(last, axis=0), jnp.concatenate(first, axis=0)
    )
    return jnp.concatenate([edge, jnp.concatenate(sides, axis=0)], axis=1)


def write_messages(z, tile, piece, message_refs):
    inside = lax.broadcasted_iota(jnp.int32, (z.fields, z.message), 1) < z.chunk
    rest = jnp.zeros((z.fields, z.message - LANES), jnp.float32)
    sides = jnp.concatenate([piece[:, z.columns :], rest], axis=1)
    for k, ref in zip(z.order, message_refs):
        shift = lax.rem(z.columns - z.target(tile, k) * z.chunk, z.columns)
        part = pltpu.roll(piece[:, : z.columns], shift, 1)[:, : z.message]
        ref[...] = jnp.where(inside, part, pltpu.roll(sides, z.chunk + 2 * z.rows * k, 1))


def start_kernel(z, state_ref, target_ref, donor_ref, weight_ref, *refs):
    messages, lists = refs[: z.tiles], refs[z.tiles : z.tiles + 3]
    first_ref, last_ref, left_ref, right_ref, sems = refs[z.tiles + 3 :]
    pairs = [
        (state_ref.at[:, pl.ds(0, 1), :], first_ref),
        (state_ref.at[:, pl.ds(z.rows - 1, 1), :], last_ref),
        (state_ref.at[:, :, pl.ds(0, LANES)], left_ref),
        (state_ref.at[:, :, pl.ds(z.columns - LANES, LANES)], right_ref),
        (target_ref, lists[0]),
        (donor_ref, lists[1]),
        (weight_ref, lists[2]),
    ]
    copies = [pltpu.make_async_copy(a, b, sems.at[i]) for i, (a, b) in enumerate(pairs)]
    for copy in copies:
        copy.start()
    tile = lax.axis_index("hor")
    for copy in copies:
        copy.wait()
    first = [first_ref[f] for f in range(z.fields)]
    last = [last_ref[f] for f in range(z.fields)]
    left = [left_ref[f][:, 0:1] for f in range(z.fields)]
    right = [right_ref[f][:, LANES - 1 : LANES] for f in range(z.fields)]
    write_messages(z, tile, border_piece(z, tile, first, last, left, right), messages)


def scatter(z, table, pick_ref, place_ref, spread_ref):
    count = table.shape[0]
    parts = [table[:, i : i + LANES] for i in range(0, z.table, LANES)]
    picked = []
    for j in range(0, z.padded, LANES):
        high, low = pick_ref[0, :, j : j + LANES], pick_ref[1, :, j : j + LANES]
        total = jnp.zeros((count, LANES), jnp.float32)
        for i, part in enumerate(parts):
            total = jnp.where(high == i, jnp.take_along_axis(part, low, axis=1), total)
        picked.append(total)
    picked = jnp.concatenate(picked, axis=1)
    spread = [spread_ref[0], spread_ref[1]]
    left = jnp.concatenate(
        [picked[f : f + 1, :] * spread[b] for b in range(2) for f in range(count)], axis=0
    )
    high, low = split(left)
    half = count * z.rows
    product = lax.dot_general(
        jnp.concatenate([high, low], axis=0),
        place_ref[...],
        (((1,), (1,)), ((), ())),
        preferred_element_type=jnp.float32,
    )
    product = product[: 2 * half] + product[2 * half :]
    added = product[:half] + pltpu.roll(product[half:], 1, 1)
    return [added[f * z.rows : (f + 1) * z.rows] for f in range(count)]


def border_mask(z, tile):
    row = lax.broadcasted_iota(jnp.int32, (z.rows, z.columns), 0)
    column = lax.broadcasted_iota(jnp.int32, (z.rows, z.columns), 1)
    return (
        ((row == 0) & (tile == 0))
        | ((row == z.rows - 1) & (tile == z.tiles - 1))
        | (column == 0)
        | (column == z.columns - 1)
    )


def read_messages(z, tile, messages):
    shape = messages[0].shape
    inside = lax.broadcasted_iota(jnp.int32, shape, 1) < z.chunk
    first = jnp.zeros(shape, jnp.float32)
    last = jnp.zeros((shape[0], z.edge), jnp.float32)
    for k, ref in zip(z.order, messages):
        message = ref[...]
        use = jnp.where(z.turn(0, tile) == k, 1, 0)
        first = first + jnp.where(inside & (use == 0), 0.0, message)
        last = jnp.where(z.turn(z.tiles - 1, tile) == k, message[:, : z.edge], last)
    return jnp.concatenate([first, last], axis=1)


def table_kernel(z, _, *refs):
    refs[-1][...] = read_messages(z, lax.axis_index("hor"), refs[:-1])


def overset_kernel(z, early, *refs):
    inputs = 2 if early else 4 + z.tiles
    given, (pick_ref, place_ref, spread_ref) = refs[:inputs], refs[inputs : inputs + 3]
    out_ref, ahead_ref, behind_ref = refs[inputs + 3 :]
    tile = lax.axis_index("hor")
    table = given[1][...] if early else read_messages(z, tile, given[4:])
    added = scatter(z, table, pick_ref, place_ref, spread_ref)
    border = border_mask(z, tile)
    even = lax.rem(tile, 2) == 0
    for f in range(z.fields):
        if early:
            value = given[0][f]
        else:
            base_ref, constant_ref, one_ref, two_ref = given[:4]
            value = finished(z, 0, f, constant_ref, base_ref[f], one_ref[f], two_ref[f])
        value = jnp.where(border, 0.0, value) + added[f]
        out_ref[f] = value
        first_row, last_row = value[0:1, :], value[z.rows - 1 : z.rows, :]
        ahead_ref[f : f + 1, :] = jnp.where(even, last_row, first_row)
        behind_ref[f : f + 1, :] = jnp.where(even, first_row, last_row)


def radial_overset_kernel(z, column_ref, one_ref, two_ref, pick_ref, place_ref, spread_ref, out_ref):
    copies = z.table // LANES
    one, two = [jnp.concatenate([column_ref[side]] * copies, axis=1) for side in range(2)]
    table = one * one_ref[...] + two * two_ref[...]
    for f, value in enumerate(scatter(z, table, pick_ref, place_ref, spread_ref)):
        out_ref[f] = value


def local_kernel(
    z,
    final,
    constant_ref,
    state_ref,
    row_one_ref,
    row_two_ref,
    diffuse_ref,
    theta_ref,
    phi_ref,
    *refs,
):
    tile = lax.axis_index("hor")
    even = lax.rem(tile, 2) == 0
    row_one, row_two = row_one_ref[...], row_two_ref[...]
    below_row = jnp.where(tile > 0, jnp.where(even, row_two, row_one), 0.0)
    above_row = jnp.where(tile < z.tiles - 1, jnp.where(even, row_one, row_two), 0.0)
    row = lax.broadcasted_iota(jnp.int32, (z.rows, z.columns), 0)
    column = lax.broadcasted_iota(jnp.int32, (z.rows, z.columns), 1)
    diffuse = diffuse_ref[...]
    theta = theta_ref[...]
    phi = phi_ref[...]
    north = diffuse + theta
    south = diffuse - theta
    east = jnp.where(column == z.columns - 1, 0.0, diffuse + phi)
    west = jnp.where(column == 0, 0.0, diffuse - phi)
    center = 4.0 * diffuse
    extra_ref, out_ref, *message_refs = refs
    step = 0.5 * STEP_SIZE if final else STEP_SIZE

    def constant(index):
        return spread(constant_ref[index], (z.rows, z.columns))

    values = []
    for f in range(z.fields):
        v = state_ref[f]
        before = jnp.where(row == 0, below_row[f : f + 1, :], pltpu.roll(v, 1, 0))
        after = jnp.where(
            row == z.rows - 1, above_row[f : f + 1, :], pltpu.roll(v, z.rows - 1, 0)
        )
        total = south * before + north * after + (constant(z.fields * z.fields + f) - center) * v
        total = total + west * pltpu.roll(v, 1, 1) + east * pltpu.roll(v, z.columns - 1, 1)
        for e in range(z.fields):
            total = total + constant(e * z.fields + f) * state_ref[e]
        total = extra_ref[f] + step * total
        if final:
            total = total + v
        out_ref[f] = total
        values.append(total)
    if not final:
        first = [v[0:1, :] for v in values]
        last = [v[z.rows - 1 : z.rows, :] for v in values]
        left = [v[:, 0:1] for v in values]
        right = [v[:, z.columns - 1 : z.columns] for v in values]
        piece = border_piece(z, tile, first, last, left, right)
        write_messages(z, tile, piece, message_refs)


def finish_kernel(z, base_ref, constant_ref, one_ref, two_ref, out_ref, held_ref, sems):
    copies = []
    for f in range(z.fields):
        held_ref[f] = finished(z, 1, f, constant_ref, base_ref[f], one_ref[f], two_ref[f])
        copies.append(pltpu.make_async_copy(held_ref.at[f], out_ref.at[f], sems.at[f]))
        copies[-1].start()
    for copy in copies:
        copy.wait()


def partners(count, odd):
    out = []
    for i in range(count):
        j = ((i + odd) ^ 1) - odd
        out.append(j if 0 <= j < count else i)
    return out


def body(
    final_cotangent,
    diffusivity,
    theta_velocity,
    phi_velocity,
    radial_stencil,
    field_coupling,
    slot_targets,
    slot_donors,
    slot_weights,
    slot_counts,
):
    fields, levels, rows, columns = final_cotangent.shape[1:]
    tiles = lax.axis_size("hor")
    z = Sizes(fields, rows, columns, tiles, lax.axis_size("rad"), slot_targets.shape[-1])
    tile = lax.axis_index("hor")
    f32 = jnp.float32

    def call(kernel, outs, in_specs, limit, scratch=(), out_spec=VMEM):
        return pl.pallas_call(
            kernel,
            out_shape=tuple(jax.ShapeDtypeStruct(shape, dtype) for shape, dtype in outs),
            in_specs=in_specs,
            out_specs=tuple(out_spec for _ in outs),
            scratch_shapes=scratch,
            compiler_params=pltpu.CompilerParams(vmem_limit_bytes=limit << 20),
        )

    def meet_levels(x, mixed):
        count = lax.axis_size("rad")
        found = []
        for turn in range(2):
            pairs = []
            for p in range(2):
                for i, j in enumerate(partners(count, p ^ turn if mixed else turn)):
                    for t in range(tiles):
                        q, u = p, t
                        if i == j and not mixed:
                            q = 1 - p
                        elif i == j:
                            beside = t ^ (1 if turn or tiles % 4 else 2)
                            u = beside if beside < tiles else t
                        pairs.append(((p * count + i) * tiles + t, (q * count + j) * tiles + u))
            found.append(lax.ppermute(x, ("panel", "rad", "hor"), pairs))
        return found

    def meet_rows(ahead, behind):
        found = []
        for odd, x in enumerate((ahead, behind)):
            pairs = [
                (p * tiles + i, (p ^ (i == j)) * tiles + j)
                for p in range(2)
                for i, j in enumerate(partners(tiles, odd))
            ]
            found.append(lax.ppermute(x, ("panel", "hor"), pairs))
        return found

    def exchange(messages):
        if tiles <= PERMUTED_TILES:
            received = []
            for k, m in zip(z.order, messages):
                pairs = [
                    (p * tiles + t, (1 - p) * tiles + z.target(t, k))
                    for p in range(2)
                    for t in range(tiles)
                ]
                received.append(lax.ppermute(m, ("panel", "hor"), pairs))
            return received
        places = jnp.arange(tiles, dtype=jnp.int32)
        stacked = jnp.stack(messages)[tiles - 1 - z.turn(tile, places)]
        stacked = lax.all_to_all(stacked, "hor", 0, 0, tiled=True)
        stacked = lax.ppermute(stacked, "panel", [(0, 1), (1, 0)])[z.source(tile, places)]
        return [stacked[k] for k in z.order]

    radial = jnp.transpose(radial_stencil, (0, 2, 1))
    coefficients = (diffusivity[0, 0], theta_velocity[0, 0], phi_velocity[0, 0])

    block = ((fields, rows, columns), f32)
    line = ((fields, columns), f32)

    def in_hbm(x):
        return pltpu.with_memory_space_constraint(x, pltpu.HBM)

    def local_part(final, state, rows_met, extra):
        sent = [] if final else [((fields, z.message), f32)] * tiles
        base, *messages = call(
            functools.partial(local_kernel, z, final), [block] + sent, [VMEM] * 8, 8
        )(constants, state, *rows_met, *coefficients, extra)
        return base, messages

    state = final_cotangent.reshape(fields, rows, columns)
    slot_line = (1, z.slots)
    row_piece = pltpu.VMEM((fields, 1, columns), f32)
    side_piece = pltpu.VMEM((fields, rows, LANES), f32)
    started = call(
        functools.partial(start_kernel, z),
        [((fields, z.message), f32)] * tiles
        + [(slot_line, jnp.int32), (slot_line, jnp.int32), (slot_line, f32)],
        [HBM] * 4,
        4,
        [row_piece, row_piece, side_piece, side_piece, pltpu.SemaphoreType.DMA((7,))],
    )(in_hbm(state), in_hbm(slot_targets[0]), in_hbm(slot_donors[0]), in_hbm(slot_weights[0]))
    received = exchange(started[:tiles])
    *maps, held, constants, factor_columns = call(
        functools.partial(prepare_kernel, z),
        [
            ((2, fields, z.padded), jnp.int32),
            ((columns, z.padded), jnp.bfloat16),
            ((2, rows, z.padded), f32),
            block,
            ((z.constants, rows, LANES), f32),
            ((2, fields, LANES), f32),
        ],
        [SMEM] + [VMEM] * 3 + [HBM] * 3,
        12,
        [
            pltpu.SMEM(radial.shape, f32),
            pltpu.SMEM(field_coupling.shape, f32),
            pltpu.SemaphoreType.DMA((3,)),
        ],
    )(slot_counts, *started[tiles:], in_hbm(state), in_hbm(radial), in_hbm(field_coupling))
    (table,) = call(
        functools.partial(table_kernel, z), [((fields, z.table), f32)], [VMEM] * (1 + tiles), 4
    )(factor_columns, *received)
    tables = meet_levels(table, False)
    levels = meet_levels(state, False)
    after_full, ahead, behind = call(
        functools.partial(overset_kernel, z, True), [block, line, line], [VMEM] * 5, 8
    )(held, table, *maps)
    rows_met = meet_rows(ahead, behind)
    (radial_added,) = call(
        functools.partial(radial_overset_kernel, z), [block], [VMEM] * 6, 8
    )(factor_columns, *tables, *maps)
    base, messages = local_part(False, after_full, rows_met, radial_added)

    received = exchange(messages)
    after_half, ahead, behind = call(
        functools.partial(overset_kernel, z, False),
        [block, line, line],
        [VMEM] * (7 + tiles),
        8,
    )(base, constants, *levels, *received, *maps)
    levels = meet_levels(after_half, True)
    base, _ = local_part(True, after_half, meet_rows(ahead, behind), after_full)
    (result,) = call(
        functools.partial(finish_kernel, z),
        [block],
        [VMEM] * 4,
        4,
        [pltpu.VMEM(*block), pltpu.SemaphoreType.DMA((fields,))],
        HBM,
    )(base, constants, *levels)
    return result.reshape(final_cotangent.shape)


def solution(mesh):
    return jax.shard_map(
        body,
        mesh=mesh,
        in_specs=(
            P("panel", None, "rad", "hor", None),
            P("panel", "rad", "hor", None),
            P("panel", "rad", "hor", None),
            P("panel", "rad", "hor", None),
            P(),
            P(),
            P("panel", "hor", None),
            P("panel", "hor", None),
            P("panel", "hor", None),
            P("panel", "hor"),
        ),
        out_specs=P("panel", None, "rad", "hor", None),
        check_vma=False,
    )
```

```python
import functools

import jax
import jax.numpy as jnp
from jax import lax
from jax.experimental import pallas as pl
from jax.experimental.pallas import tpu as pltpu
from jax.sharding import PartitionSpec as P

STEP_SIZE = 0.2
LANES = 128
PERMUTED_TILES = 8
VMEM = pl.BlockSpec(memory_space=pltpu.VMEM)
HBM = pl.BlockSpec(memory_space=pltpu.HBM)
SMEM = pl.BlockSpec(memory_space=pltpu.SMEM)


def round_up(n, m):
    return -(-n // m) * m


class Sizes:
    def __init__(self, fields, rows, columns, tiles, levels, slots):
        self.fields, self.rows, self.columns, self.tiles = fields, rows, columns, tiles
        self.levels = levels
        self.chunk = columns // tiles
        self.edge = round_up(self.chunk, LANES)
        self.message = round_up(self.chunk + 2 * rows * tiles, LANES)
        self.table = self.message + self.edge
        self.paired = tiles & (tiles - 1) == 0
        self.constants = fields * (fields + 5)
        self.order = list(reversed(range(tiles)))
        self.slots = slots
        self.groups = slots // 4
        self.padded = round_up(self.groups, LANES)


    def factor(self, final, f, side):
        return self.fields * (self.fields + 1 + 2 * final) + 2 * f + side

    def target(self, source, k):
        return source ^ k if self.paired else (source + k) % self.tiles

    def source(self, target, k):
        return target ^ k if self.paired else (target - k) % self.tiles

    def turn(self, source, target):
        return source ^ target if self.paired else (target - source) % self.tiles


def split(x):
    high = x.astype(jnp.bfloat16)
    low = (x - high.astype(jnp.float32)).astype(jnp.bfloat16)
    return high, low


def pieces(x, count):
    out = []
    for _ in range(count):
        out.append(x.astype(jnp.bfloat16).astype(jnp.float32))
        x = x - out[-1]
    return out


def write_hits(z, index, out_ref):
    bf16 = jnp.bfloat16
    high = index >> 7
    low = index - (high << 7)
    own = lax.broadcasted_iota(jnp.int32, (LANES, LANES), 0).astype(bf16)
    one, zero = jnp.ones((LANES, LANES), bf16), jnp.zeros((LANES, LANES), bf16)
    for i in range(0, out_ref.shape[0], LANES):
        inside = jnp.where(high == i // LANES, low, -1).astype(bf16)
        for j in range(0, z.padded, LANES):
            hit = own == inside[:, j : j + LANES]
            out_ref[i : i + LANES, j : j + LANES] = jnp.where(hit, one, zero)


def write_constants(z, radial_ref, coupling_ref, constant_ref, column_ref):
    level = lax.axis_index("rad")
    below = jnp.maximum(level - 1, 0)
    above = jnp.minimum(level + 1, z.levels - 1)
    first_above = (lax.rem(level, 2) == 0, lax.rem(level + lax.axis_index("panel"), 2) == 0)
    row = lax.broadcasted_iota(jnp.int32, (z.fields, LANES), 0)
    columns = [jnp.zeros((z.fields, LANES), jnp.float32)] * 2

    def write(index, value):
        constant_ref[index] = jnp.full((z.rows, LANES), value, jnp.float32)

    for f in range(z.fields):
        for e in range(z.fields):
            write(e * z.fields + f, coupling_ref[level, e, f])
        write(z.fields * z.fields + f, radial_ref[0, level, f])
        upper = jnp.where(level > 0, radial_ref[1, below, f], 0.0)
        lower = jnp.where(level < z.levels - 1, radial_ref[2, above, f], 0.0)
        for final, above_first in enumerate(first_above):
            step = 0.5 * STEP_SIZE if final else STEP_SIZE
            factors = [
                step * jnp.where(above_first, lower, upper),
                step * jnp.where(above_first, upper, lower),
            ]
            for side, factor in enumerate(factors):
                write(z.factor(final, f, side), factor)
            if not final:
                columns = [jnp.where(row == f, a, b) for a, b in zip(factors, columns)]
    for side, column in enumerate(columns):
        column_ref[side] = column


def spread(constant, shape):
    return jnp.concatenate([constant[: shape[0]]] * (shape[1] // LANES), axis=1)


def finished(z, final, f, constant_ref, base, one, two):
    factors = [spread(constant_ref[z.factor(final, f, side)], base.shape) for side in range(2)]
    return base + factors[0] * one + factors[1] * two


def prepare_kernel(z, *refs):
    count_ref, target_ref, donor_ref, weight_ref = refs[:4]
    sources, (pick_ref, place_ref, spread_ref, held_ref, constant_ref, column_ref) = (
        refs[4:7],
        refs[7:13],
    )
    radial_ref, coupling_ref, sems = refs[13:]
    copies = [
        pltpu.make_async_copy(source, target, sems.at[i])
        for i, (source, target) in enumerate(zip(sources, (held_ref, radial_ref, coupling_ref)))
    ]
    for copy in copies:
        copy.start()
    f32 = jnp.float32
    slot = lax.broadcasted_iota(jnp.int32, (1, z.slots), 1)
    weight = jnp.where(slot < count_ref[0, 0], weight_ref[...], 0.0)
    tile = lax.axis_index("hor")
    lists = pieces(target_ref[...].astype(f32), 2)
    lists += pieces(donor_ref[...].astype(f32), 2) + pieces(weight, 3)
    lists = jnp.concatenate(lists + [jnp.zeros((1, z.slots), f32)], axis=0)
    blocks = -(-z.slots // 256)
    if blocks * 256 > z.slots:
        tail = jnp.zeros((8, blocks * 256 - z.slots), f32)
        lists = jnp.concatenate([lists, tail], axis=1)
    stacked = jnp.concatenate([lists[:, 256 * b : 256 * (b + 1)] for b in range(blocks)], axis=0)
    lane_in = lax.broadcasted_iota(jnp.int32, (256, 256), 0)
    lane_out = lax.broadcasted_iota(jnp.int32, (256, 256), 1)
    move = jnp.where(lane_out == 64 * (lane_in & 3) + (lane_in >> 2), 1.0, 0.0)
    moved = jnp.dot(
        stacked.astype(jnp.bfloat16), move.astype(jnp.bfloat16), preferred_element_type=f32
    )
    quarter = []
    for q in range(4):
        parts = [moved[8 * b : 8 * (b + 1), 64 * q : 64 * (q + 1)] for b in range(blocks)]
        if z.padded > 64 * blocks:
            parts.append(jnp.zeros((8, z.padded - 64 * blocks), f32))
        quarter.append(jnp.concatenate(parts, axis=1)[:, : z.padded])
    group = lax.broadcasted_iota(jnp.int32, (1, z.padded), 1)
    target = quarter[0][0:1] + quarter[0][1:2]
    donors = [x[2:3] + x[3:4] for x in quarter]
    weights = [x[4:5] + x[5:6] + x[6:7] for x in quarter]

    def row_of(cell):
        row = jnp.zeros_like(cell)
        for i in range(1, z.rows):
            row = row + jnp.where(cell >= float(i * z.columns), 1.0, 0.0)
        return row

    base = jnp.minimum(jnp.minimum(donors[0], donors[1]), jnp.minimum(donors[2], donors[3]))
    base_column = base - row_of(base) * z.columns
    base_column = jnp.where(group < z.groups, base_column, -1.0).astype(jnp.int32)
    target = target.astype(jnp.int32)
    total_rows = z.rows * z.tiles
    along = target - 2 * z.columns
    side = jnp.where(along >= total_rows, 1, 0)
    side_row = along - total_rows * side
    owner = jnp.floor((side_row.astype(f32) + 0.5) * (1.0 / z.rows)).astype(jnp.int32)
    if z.paired:
        turn = jnp.full_like(owner, tile) ^ owner
    else:
        turn = tile - owner + jnp.where(owner > tile, z.tiles, 0)
    side_place = z.chunk + 2 * z.rows * turn + z.rows * (side - owner) + side_row
    edge_place = target - tile * z.chunk
    local = jnp.where(
        target < z.columns,
        edge_place,
        jnp.where(target < 2 * z.columns, edge_place + z.message - z.columns, side_place),
    )
    local = jnp.where(group < z.groups, local, -1)
    high = local >> 7
    pick_ref[0] = jnp.broadcast_to(high, (z.fields, z.padded))
    pick_ref[1] = jnp.broadcast_to(local - (high << 7), (z.fields, z.padded))
    write_hits(z, base_column, place_ref)
    rows = lax.broadcasted_iota(jnp.int32, (z.rows, z.padded), 0)
    for b in range(2):
        total = jnp.zeros((z.rows, z.padded), f32)
        for donor, weight in zip(donors, weights):
            row = row_of(donor)
            column = donor.astype(jnp.int32) - row.astype(jnp.int32) * z.columns
            hit = (rows == row.astype(jnp.int32)) & (column == base_column + b)
            total = total + jnp.where(hit, weight, 0.0)
        spread_ref[b] = total
    for copy in copies:
        copy.wait()
    write_constants(z, radial_ref, coupling_ref, constant_ref, column_ref)


def border_piece(z, tile, first, last, left, right):
    lane = lax.broadcasted_iota(jnp.int32, (z.rows, LANES), 1)
    row = lax.broadcasted_iota(jnp.int32, (z.rows, LANES), 0)
    sides = []
    for f in range(z.fields):
        one = jnp.where(lane == row, left[f], 0.0)
        two = jnp.where(lane == row + z.rows, right[f], 0.0)
        sides.append(jnp.sum(one + two, axis=0, keepdims=True))
    edge = jnp.where(
        tile == z.tiles - 1, jnp.concatenate(last, axis=0), jnp.concatenate(first, axis=0)
    )
    return jnp.concatenate([edge, jnp.concatenate(sides, axis=0)], axis=1)


def write_messages(z, tile, piece, message_refs):
    inside = lax.broadcasted_iota(jnp.int32, (z.fields, z.message), 1) < z.chunk
    rest = jnp.zeros((z.fields, z.message - LANES), jnp.float32)
    sides = jnp.concatenate([piece[:, z.columns :], rest], axis=1)
    for k, ref in zip(z.order, message_refs):
        shift = lax.rem(z.columns - z.target(tile, k) * z.chunk, z.columns)
        part = pltpu.roll(piece[:, : z.columns], shift, 1)[:, : z.message]
        ref[...] = jnp.where(inside, part, pltpu.roll(sides, z.chunk + 2 * z.rows * k, 1))


def start_kernel(z, state_ref, target_ref, donor_ref, weight_ref, *refs):
    messages, lists = refs[: z.tiles], refs[z.tiles : z.tiles + 3]
    first_ref, last_ref, left_ref, right_ref, sems = refs[z.tiles + 3 :]
    pairs = [
        (state_ref.at[:, pl.ds(0, 1), :], first_ref),
        (state_ref.at[:, pl.ds(z.rows - 1, 1), :], last_ref),
        (state_ref.at[:, :, pl.ds(0, LANES)], left_ref),
        (state_ref.at[:, :, pl.ds(z.columns - LANES, LANES)], right_ref),
        (target_ref, lists[0]),
        (donor_ref, lists[1]),
        (weight_ref, lists[2]),
    ]
    copies = [pltpu.make_async_copy(a, b, sems.at[i]) for i, (a, b) in enumerate(pairs)]
    for copy in copies:
        copy.start()
    tile = lax.axis_index("hor")
    for copy in copies:
        copy.wait()
    first = [first_ref[f] for f in range(z.fields)]
    last = [last_ref[f] for f in range(z.fields)]
    left = [left_ref[f][:, 0:1] for f in range(z.fields)]
    right = [right_ref[f][:, LANES - 1 : LANES] for f in range(z.fields)]
    write_messages(z, tile, border_piece(z, tile, first, last, left, right), messages)


def scatter(z, table, pick_ref, place_ref, spread_ref, low=0, end=None):
    end = end or z.columns
    begin = max(low - LANES, 0)
    count = table.shape[0]
    parts = [table[:, i : i + LANES] for i in range(0, z.table, LANES)]
    picked = []
    for j in range(0, z.padded, LANES):
        which, lane = pick_ref[0, :, j : j + LANES], pick_ref[1, :, j : j + LANES]
        total = jnp.zeros((count, LANES), jnp.float32)
        for i, part in enumerate(parts):
            total = jnp.where(which == i, jnp.take_along_axis(part, lane, axis=1), total)
        picked.append(total)
    picked = jnp.concatenate(picked, axis=1)
    spread = [spread_ref[0], spread_ref[1]]
    left = jnp.concatenate(
        [picked[f : f + 1, :] * spread[b] for b in range(2) for f in range(count)], axis=0
    )
    pair = jnp.concatenate(split(left), axis=0)
    half = count * z.rows
    product = lax.dot_general(
        pair,
        place_ref[begin:end, :],
        (((1,), (1,)), ((), ())),
        preferred_element_type=jnp.float32,
    )
    product = product[: 2 * half] + product[2 * half :]
    moved = pltpu.roll(product[half:], 1, 1)
    if begin == 0 and end < z.columns:
        moved = jnp.where(lax.broadcasted_iota(jnp.int32, moved.shape, 1) == 0, 0.0, moved)
    added = (product[:half] + moved)[:, low - begin :]
    return [added[f * z.rows : (f + 1) * z.rows] for f in range(count)]


def border_mask(z, tile, low=0, end=None):
    shape = (z.rows, (end or z.columns) - low)
    row = lax.broadcasted_iota(jnp.int32, shape, 0)
    column = lax.broadcasted_iota(jnp.int32, shape, 1) + low
    return (
        ((row == 0) & (tile == 0))
        | ((row == z.rows - 1) & (tile == z.tiles - 1))
        | (column == 0)
        | (column == z.columns - 1)
    )


def read_messages(z, tile, messages):
    shape = messages[0].shape
    inside = lax.broadcasted_iota(jnp.int32, shape, 1) < z.chunk
    first = jnp.zeros(shape, jnp.float32)
    last = jnp.zeros((shape[0], z.edge), jnp.float32)
    for k, ref in zip(z.order, messages):
        message = ref[...]
        use = jnp.where(z.turn(0, tile) == k, 1, 0)
        first = first + jnp.where(inside & (use == 0), 0.0, message)
        last = jnp.where(z.turn(z.tiles - 1, tile) == k, message[:, : z.edge], last)
    return jnp.concatenate([first, last], axis=1)


def table_kernel(z, _, *refs):
    refs[-1][...] = read_messages(z, lax.axis_index("hor"), refs[:-1])


def write_rows(even, f, value, ahead_ref, behind_ref, low=0):
    first, last = value[0:1, :], value[value.shape[0] - 1 :, :]
    place = (slice(f, f + 1), slice(low, low + value.shape[1]))
    ahead_ref[place] = jnp.where(even, last, first)
    behind_ref[place] = jnp.where(even, first, last)


def overset_kernel(z, state_ref, table_ref, pick_ref, place_ref, spread_ref, *outs):
    out_ref, ahead_ref, behind_ref = outs
    tile = lax.axis_index("hor")
    added = scatter(z, table_ref[...], pick_ref, place_ref, spread_ref)
    border = border_mask(z, tile)
    even = lax.rem(tile, 2) == 0
    for f in range(z.fields):
        value = jnp.where(border, 0.0, state_ref[f]) + added[f]
        out_ref[f] = value
        write_rows(even, f, value, ahead_ref, behind_ref)


def late_overset_kernel(z, low, end, base_ref, constant_ref, one_ref, two_ref, *refs):
    messages, (pick_ref, place_ref, spread_ref) = refs[: z.tiles], refs[z.tiles : z.tiles + 3]
    rest = refs[z.tiles + 3 :]
    tile = lax.axis_index("hor")
    table = read_messages(z, tile, messages)
    added = scatter(z, table, pick_ref, place_ref, spread_ref, low, end)
    border = border_mask(z, tile, low, end)
    even = lax.rem(tile, 2) == 0
    if low:
        part_ref, out_ref, ahead_ref, behind_ref = rest
    else:
        (out_ref,) = rest
    for f in range(z.fields):
        place = (f, slice(None), slice(low, end))
        value = finished(z, 0, f, constant_ref, base_ref[place], one_ref[place], two_ref[place])
        value = jnp.where(border, 0.0, value) + added[f]
        out_ref[f] = value
        if low:
            write_rows(even, f, part_ref[f], ahead_ref, behind_ref)
            write_rows(even, f, value, ahead_ref, behind_ref, low)


def radial_overset_kernel(z, column_ref, one_ref, two_ref, pick_ref, place_ref, spread_ref, out_ref):
    copies = z.table // LANES
    one, two = [jnp.concatenate([column_ref[side]] * copies, axis=1) for side in range(2)]
    table = one * one_ref[...] + two * two_ref[...]
    for f, value in enumerate(scatter(z, table, pick_ref, place_ref, spread_ref)):
        out_ref[f] = value


def local_kernel(z, final, constant_ref, *refs):
    parts = 2 if final else 1
    state_refs, refs = refs[:parts], refs[parts:]
    row_one_ref, row_two_ref, diffuse_ref, theta_ref, phi_ref, *refs = refs
    state = [jnp.concatenate([ref[f] for ref in state_refs], axis=1) for f in range(z.fields)]
    tile = lax.axis_index("hor")
    even = lax.rem(tile, 2) == 0
    row_one, row_two = row_one_ref[...], row_two_ref[...]
    below_row = jnp.where(tile > 0, jnp.where(even, row_two, row_one), 0.0)
    above_row = jnp.where(tile < z.tiles - 1, jnp.where(even, row_one, row_two), 0.0)
    row = lax.broadcasted_iota(jnp.int32, (z.rows, z.columns), 0)
    column = lax.broadcasted_iota(jnp.int32, (z.rows, z.columns), 1)
    diffuse = diffuse_ref[...]
    theta = theta_ref[...]
    phi = phi_ref[...]
    north = diffuse + theta
    south = diffuse - theta
    east = jnp.where(column == z.columns - 1, 0.0, diffuse + phi)
    west = jnp.where(column == 0, 0.0, diffuse - phi)
    center = 4.0 * diffuse
    extra_ref, out_ref, *message_refs = refs
    step = 0.5 * STEP_SIZE if final else STEP_SIZE

    def constant(index):
        return spread(constant_ref[index], (z.rows, z.columns))

    values = []
    for f in range(z.fields):
        v = state[f]
        before = jnp.where(row == 0, below_row[f : f + 1, :], pltpu.roll(v, 1, 0))
        after = jnp.where(
            row == z.rows - 1, above_row[f : f + 1, :], pltpu.roll(v, z.rows - 1, 0)
        )
        total = south * before + north * after + (constant(z.fields * z.fields + f) - center) * v
        total = total + west * pltpu.roll(v, 1, 1) + east * pltpu.roll(v, z.columns - 1, 1)
        for e in range(z.fields):
            total = total + constant(e * z.fields + f) * state[e]
        total = extra_ref[f] + step * total
        if final:
            total = total + v
        out_ref[f] = total
        values.append(total)
    if not final:
        first = [v[0:1, :] for v in values]
        last = [v[z.rows - 1 : z.rows, :] for v in values]
        left = [v[:, 0:1] for v in values]
        right = [v[:, z.columns - 1 : z.columns] for v in values]
        piece = border_piece(z, tile, first, last, left, right)
        write_messages(z, tile, piece, message_refs)


def finish_kernel(z, cut, base_ref, constant_ref, *refs):
    (one_a, two_a, one_b, two_b), (out_ref, held_ref, sems) = refs[:4], refs[4:]
    copies = []
    for f in range(z.fields):
        a = (f, slice(None), slice(0, cut))
        b = (f, slice(None), slice(cut, z.columns))
        held_ref[a] = finished(z, 1, f, constant_ref, base_ref[a], one_a[f], two_a[f])
        held_ref[b] = finished(z, 1, f, constant_ref, base_ref[b], one_b[f], two_b[f])
        copies.append(pltpu.make_async_copy(held_ref.at[f], out_ref.at[f], sems.at[f]))
        copies[-1].start()
    for copy in copies:
        copy.wait()


def partners(count, odd):
    out = []
    for i in range(count):
        j = ((i + odd) ^ 1) - odd
        out.append(j if 0 <= j < count else i)
    return out


def body(
    final_cotangent,
    diffusivity,
    theta_velocity,
    phi_velocity,
    radial_stencil,
    field_coupling,
    slot_targets,
    slot_donors,
    slot_weights,
    slot_counts,
):
    fields, levels, rows, columns = final_cotangent.shape[1:]
    tiles = lax.axis_size("hor")
    z = Sizes(fields, rows, columns, tiles, lax.axis_size("rad"), slot_targets.shape[-1])
    tile = lax.axis_index("hor")
    f32 = jnp.float32

    def call(kernel, outs, in_specs, limit, scratch=(), out_spec=VMEM):
        return pl.pallas_call(
            kernel,
            out_shape=tuple(jax.ShapeDtypeStruct(shape, dtype) for shape, dtype in outs),
            in_specs=in_specs,
            out_specs=tuple(out_spec for _ in outs),
            scratch_shapes=scratch,
            compiler_params=pltpu.CompilerParams(vmem_limit_bytes=limit << 20),
        )

    def meet_levels(x, mixed):
        count = lax.axis_size("rad")
        found = []
        for turn in range(2):
            pairs = []
            for p in range(2):
                for i, j in enumerate(partners(count, p ^ turn if mixed else turn)):
                    for t in range(tiles):
                        q, u = p, t
                        if i == j and not mixed:
                            q = 1 - p
                        elif i == j:
                            beside = t ^ (1 if turn or tiles % 4 else 2)
                            u = beside if beside < tiles else t
                        pairs.append(((p * count + i) * tiles + t, (q * count + j) * tiles + u))
            found.append(lax.ppermute(x, ("panel", "rad", "hor"), pairs))
        return found

    def meet_rows(ahead, behind):
        found = []
        for odd, x in enumerate((ahead, behind)):
            pairs = [
                (p * tiles + i, (p ^ (i == j)) * tiles + j)
                for p in range(2)
                for i, j in enumerate(partners(tiles, odd))
            ]
            found.append(lax.ppermute(x, ("panel", "hor"), pairs))
        return found

    def exchange(messages):
        if tiles <= PERMUTED_TILES:
            received = []
            for k, m in zip(z.order, messages):
                pairs = [
                    (p * tiles + t, (1 - p) * tiles + z.target(t, k))
                    for p in range(2)
                    for t in range(tiles)
                ]
                received.append(lax.ppermute(m, ("panel", "hor"), pairs))
            return received
        places = jnp.arange(tiles, dtype=jnp.int32)
        stacked = jnp.stack(messages)[tiles - 1 - z.turn(tile, places)]
        stacked = lax.all_to_all(stacked, "hor", 0, 0, tiled=True)
        stacked = lax.ppermute(stacked, "panel", [(0, 1), (1, 0)])[z.source(tile, places)]
        return [stacked[k] for k in z.order]

    radial = jnp.transpose(radial_stencil, (0, 2, 1))
    coefficients = (diffusivity[0, 0], theta_velocity[0, 0], phi_velocity[0, 0])

    block = ((fields, rows, columns), f32)
    line = ((fields, columns), f32)

    def in_hbm(x):
        return pltpu.with_memory_space_constraint(x, pltpu.HBM)

    def local_part(final, state, rows_met, extra):
        sent = [] if final else [((fields, z.message), f32)] * tiles
        base, *messages = call(
            functools.partial(local_kernel, z, final), [block] + sent, [VMEM] * (7 + len(state)), 8
        )(constants, *state, *rows_met, *coefficients, extra)
        return base, messages

    state = final_cotangent.reshape(fields, rows, columns)
    slot_line = (1, z.slots)
    row_piece = pltpu.VMEM((fields, 1, columns), f32)
    side_piece = pltpu.VMEM((fields, rows, LANES), f32)
    started = call(
        functools.partial(start_kernel, z),
        [((fields, z.message), f32)] * tiles
        + [(slot_line, jnp.int32), (slot_line, jnp.int32), (slot_line, f32)],
        [HBM] * 4,
        4,
        [row_piece, row_piece, side_piece, side_piece, pltpu.SemaphoreType.DMA((7,))],
    )(in_hbm(state), in_hbm(slot_targets[0]), in_hbm(slot_donors[0]), in_hbm(slot_weights[0]))
    received = exchange(started[:tiles])
    *maps, held, constants, factor_columns = call(
        functools.partial(prepare_kernel, z),
        [
            ((2, fields, z.padded), jnp.int32),
            ((columns, z.padded), jnp.bfloat16),
            ((2, rows, z.padded), f32),
            block,
            ((z.constants, rows, LANES), f32),
            ((2, fields, LANES), f32),
        ],
        [SMEM] + [VMEM] * 3 + [HBM] * 3,
        12,
        [
            pltpu.SMEM(radial.shape, f32),
            pltpu.SMEM(field_coupling.shape, f32),
            pltpu.SemaphoreType.DMA((3,)),
        ],
    )(slot_counts, *started[tiles:], in_hbm(state), in_hbm(radial), in_hbm(field_coupling))
    (table,) = call(
        functools.partial(table_kernel, z), [((fields, z.table), f32)], [VMEM] * (1 + tiles), 4
    )(factor_columns, *received)
    tables = meet_levels(table, False)
    levels = meet_levels(state, False)
    after_full, ahead, behind = call(
        functools.partial(overset_kernel, z), [block, line, line], [VMEM] * 5, 8
    )(held, table, *maps)
    rows_met = meet_rows(ahead, behind)
    (radial_added,) = call(
        functools.partial(radial_overset_kernel, z), [block], [VMEM] * 6, 8
    )(factor_columns, *tables, *maps)
    base, messages = local_part(False, [after_full], rows_met, radial_added)

    received = exchange(messages)
    cut = round_up(columns * 5 // 9, LANES)
    given = (base, constants, *levels, *received, *maps)
    (part_a,) = call(
        functools.partial(late_overset_kernel, z, 0, cut),
        [((fields, rows, cut), f32)],
        [VMEM] * (7 + tiles),
        8,
    )(*given)
    levels_a = meet_levels(part_a, True)
    part_b, ahead, behind = call(
        functools.partial(late_overset_kernel, z, cut, columns),
        [((fields, rows, columns - cut), f32), line, line],
        [VMEM] * (8 + tiles),
        8,
    )(*given, part_a)
    levels_b = meet_levels(part_b, True)
    base, _ = local_part(True, [part_a, part_b], meet_rows(ahead, behind), after_full)
    (result,) = call(
        functools.partial(finish_kernel, z, cut),
        [block],
        [VMEM] * 6,
        4,
        [pltpu.VMEM(*block), pltpu.SemaphoreType.DMA((fields,))],
        HBM,
    )(base, constants, *levels_a, *levels_b)
    return result.reshape(final_cotangent.shape)


def solution(mesh):
    return jax.shard_map(
        body,
        mesh=mesh,
        in_specs=(
            P("panel", None, "rad", "hor", None),
            P("panel", "rad", "hor", None),
            P("panel", "rad", "hor", None),
            P("panel", "rad", "hor", None),
            P(),
            P(),
            P("panel", "hor", None),
            P("panel", "hor", None),
            P("panel", "hor", None),
            P("panel", "hor"),
        ),
        out_specs=P("panel", None, "rad", "hor", None),
        check_vma=False,
    )
```
